32 devices in a mesh: ad: 8 (over z, core), tp: 4 (over y, x).
Axes of the slice: x: 2, y: 2, z: 4, core: 2. Of those that a mesh axis runs over, the one named last changes fastest.
Arguments:
- tokens: bfloat16 [1024, 8192], P('ad', 'tp'), may hold values from -6 to 6
- query_weight: bfloat16 [8192, 8192], P(None, 'tp'), may hold values from -0.0625 to 0.0625
- adapter_down_weight: bfloat16 [128, 8192, 64], P('ad', 'tp'), may hold values from -0.0625 to 0.0625
- adapter_up_weight: bfloat16 [128, 64, 8192], P('ad', None, 'tp'), may hold values from -0.75 to 0.75
- row_adapter_index: int32 [1024], P('ad'), may hold values from 0 to 127, as said below
- adapter_table_slot: int32 [128], replicated, may hold values from 0 to 127, as said below
- lengths: int32 [1024], P('ad'), may hold values from 1 to 64, as said below
- cached_key_rows: bfloat16 [1024, 8, 64, 128], P('ad', None, 'tp'), may hold values from -360 to 360
- cached_value_rows: bfloat16 [1024, 8, 64, 128], P('ad', None, 'tp'), may hold values from -6 to 6
Outputs:
- queries: bfloat16 [1024, 8192], P('ad', 'tp')
- attended: bfloat16 [1024, 8192], P('ad', 'tp')
The draws below stay inside these ranges and needn't reach their ends.
Inputs may be any that keep to these rules, and one draw needn't show every extreme that they name: `row_adapter_index`: within each aligned block of 128 rows at most 48 rows have their adapter's slot in any one run of 16 slots (slot // 16); one such run, drawn from the seed, is named by exactly 48 rows of every block. `adapter_table_slot`: A permutation of the slots. `lengths`: some row has exactly 64 and some row exactly 1.
All inputs are finite; a program needn't handle non-finite values.
Results may differ from the reference program's by a relative error of at most 0.019.
Values may be sent and summed in bfloat16 or wider, within the bound.
A program may use at most 128 MiB of HBM per device.

```python
import math
import jax
import jax.numpy as jnp
from jax import lax

MODEL_WIDTH = 8192
QUERY_HEADS = 64
KVH = 8
HEAD_SIZE = 128
ADAPTER_RANK = 64
ADAPT_DEV = 16
ROWS_DEV = 128
POS_DEV = 16
ADAPTER_TOTAL = 128
ROWS = 1024
CTX = 64
CAP = 48
N_TP = 4


def owner_table(key):
    return jax.random.permutation(jax.random.fold_in(key, 11), ADAPTER_TOTAL).astype(jnp.int32)


def draw_adapter_table_slot(key, part):
    return owner_table(key)


def draw_row_adapter_index(key, part):
    table = owner_table(key)
    inverse = jnp.argsort(table, stable=True).astype(jnp.int32)
    blocks = ROWS // ROWS_DEV
    hottest = jax.random.randint(jax.random.fold_in(key, 12), (), 0, blocks).astype(jnp.int32)
    pool_size = (blocks - 1) * CAP

    def one_block(index):
        inner = jax.random.fold_in(jax.random.fold_in(key, 13), index)
        picks = jax.random.permutation(jax.random.fold_in(inner, 1), pool_size)[:ROWS_DEV - CAP].astype(jnp.int32)
        others = picks // CAP
        others = others + (others >= hottest).astype(jnp.int32)
        owners = jnp.concatenate([jnp.full((CAP,), 0, jnp.int32) + hottest, others])
        owners = jax.random.permutation(jax.random.fold_in(inner, 2), owners)
        local_partial = jax.random.randint(jax.random.fold_in(inner, 3), (ROWS_DEV,), 0, ADAPT_DEV).astype(jnp.int32)
        return inverse[owners * ADAPT_DEV + local_partial]
    return jax.vmap(one_block)(jnp.arange(blocks, dtype=jnp.int32)).reshape(ROWS).astype(jnp.int32)


def draw_lengths(key, part):
    values = jax.random.randint(jax.random.fold_in(key, 21), (ROWS,), 1, CTX + 1).astype(jnp.int32)
    longest = jax.random.randint(jax.random.fold_in(key, 22), (), 0, ROWS // 2)
    shortest = jax.random.randint(jax.random.fold_in(key, 23), (), ROWS // 2, ROWS)
    values = values.at[longest].set(CTX)
    return values.at[shortest].set(1)


def draw_cached_key_rows(key, part):
    values = jax.random.normal(jax.random.fold_in(key, 31), (ROWS, KVH, CTX, HEAD_SIZE), jnp.float32)
    values = jnp.clip(values, -6.0, 6.0)
    return values.astype(jnp.bfloat16)


def levels(rng, extent, cuts, least, largest):
    def one(dim, shards_of):
        steps = jax.random.uniform(jax.random.fold_in(jax.random.fold_in(rng, 6), dim), (shards_of,), jnp.float32, least / len(cuts), largest / len(cuts))
        return jnp.repeat(jnp.exp(steps), extent[dim] // shards_of).reshape((-1,) + (1,) * (len(extent) - dim - 1))

    factor_of = one(*cuts[0])
    for cut in cuts[1:]:
        factor_of = factor_of * one(*cut)
    return factor_of


def gaussian(own_key, dims, deviation, most, pieces=(), kind=jnp.bfloat16):
    loudness = levels(own_key, dims, pieces, -0.22, 0.18) if pieces else 1.0
    values = jax.random.normal(own_key, dims, jnp.float32) * deviation * loudness
    return jnp.minimum(jnp.maximum(values, -most), most).astype(kind)


def setup_inputs(seed: int = 0) -> dict:
    key_of = jax.random.split(jax.random.key(seed), 10)
    return {
        "tokens": gaussian(key_of[0], (ROWS, MODEL_WIDTH), 1.0, 6.0, ((0, 8), (1, 4))),
        "query_weight": gaussian(key_of[1], (MODEL_WIDTH, QUERY_HEADS * HEAD_SIZE), MODEL_WIDTH ** -0.5, 0.0625, ((1, 4),)),
        "adapter_down_weight": gaussian(key_of[2], (ADAPTER_TOTAL, MODEL_WIDTH, ADAPTER_RANK), MODEL_WIDTH ** -0.5, 0.0625, ((0, 8), (1, 4))),
        "adapter_up_weight": gaussian(key_of[3], (ADAPTER_TOTAL, ADAPTER_RANK, QUERY_HEADS * HEAD_SIZE), ADAPTER_RANK ** -0.5, 0.75, ((0, 8), (2, 4))),
        "row_adapter_index": draw_row_adapter_index(jax.random.fold_in(key_of[9], 71), 0),
        "adapter_table_slot": draw_adapter_table_slot(jax.random.fold_in(key_of[9], 71), 0),
        "lengths": draw_lengths(jax.random.fold_in(key_of[9], 71), 0),
        "cached_key_rows": draw_cached_key_rows(jax.random.fold_in(key_of[9], 71), 0),
        "cached_value_rows": gaussian(key_of[8], (ROWS, KVH, CTX, HEAD_SIZE), 1.0, 6.0, ((0, 8), (2, 4))),
    }


def rotate(query, lengths):
    head_dim = query.shape[-1]
    half = head_dim // 2
    freq = jnp.exp(jnp.arange(half, dtype=jnp.float32) * (-2.0 * math.log(500000.0) / head_dim))
    angle = (lengths - 1).astype(jnp.float32)[:, None, None] * freq[None, None, :]
    cosine = jnp.cos(angle)
    sine = jnp.sin(angle)
    first = query[..., :half]
    second = query[..., half:]
    return jnp.concatenate([first * cosine - second * sine, second * cosine + first * sine], axis=-1)

def reference(tokens, query_weight, adapter_down_weight, adapter_up_weight, row_adapter_index, adapter_table_slot, lengths, cached_key_rows, cached_value_rows):
    base = jnp.dot(tokens, query_weight, preferred_element_type=jnp.float32)
    slots = adapter_table_slot[row_adapter_index]

    def adapter_block(input_rows):
        rows, slot_row_table = input_rows
        down_weight = adapter_down_weight[slot_row_table].astype(jnp.float32)
        reduced_rows = jnp.einsum('rd,rdk->rk', rows.astype(jnp.float32), down_weight).astype(jnp.bfloat16)
        up_weight = adapter_up_weight[slot_row_table].astype(jnp.float32)
        return jnp.einsum('rk,rke->re', reduced_rows.astype(jnp.float32), up_weight).astype(jnp.bfloat16)
    delta = lax.map(adapter_block, (tokens.reshape(ROWS // 64, 64, MODEL_WIDTH), slots.reshape(ROWS // 64, 64)))
    delta = delta.reshape(ROWS, QUERY_HEADS * HEAD_SIZE)
    query = (base + delta.astype(jnp.float32)).reshape(ROWS, QUERY_HEADS, HEAD_SIZE)
    queries = rotate(query, lengths).reshape(ROWS, QUERY_HEADS * HEAD_SIZE).astype(jnp.bfloat16)
    scale = 1.0 / math.sqrt(HEAD_SIZE)
    group = QUERY_HEADS // KVH

    def attend_block(input_rows):
        qrows, keys, values, lens = input_rows
        grouped = qrows.reshape(64, KVH, group, HEAD_SIZE).astype(jnp.float32)
        keys = keys.reshape(64, KVH, N_TP, POS_DEV, HEAD_SIZE).astype(jnp.float32)
        values = values.reshape(64, KVH, N_TP, POS_DEV, HEAD_SIZE).astype(jnp.float32)
        scores = jnp.einsum('rkgd,rkbpd->rkgbp', grouped, keys) * scale
        position = jnp.arange(CTX, dtype=jnp.int32).reshape(N_TP, POS_DEV)
        valid = (position[None, :, :] < lens[:, None, None])[:, None, None, :, :]
        scores = jnp.where(valid, scores, -1e+30)
        peak = lax.optimization_barrier(jnp.max(scores, axis=-1))
        weights = jnp.where(valid, jnp.exp(scores - peak[..., None]), 0.0)
        total = lax.optimization_barrier(jnp.sum(weights, axis=-1))
        partial_value_sum = jnp.einsum('rkgbp,rkbpd->rkgbd', weights.astype(jnp.bfloat16).astype(jnp.float32), values).astype(jnp.bfloat16)
        top = lax.optimization_barrier(jnp.max(peak, axis=-1, keepdims=True))
        factor = jnp.exp(peak - top)
        numer = lax.optimization_barrier(jnp.sum(factor[..., None] * partial_value_sum.astype(jnp.float32), axis=3))
        denom = lax.optimization_barrier(jnp.sum(factor * total, axis=3))
        return (numer / denom[..., None]).reshape(64, QUERY_HEADS * HEAD_SIZE).astype(jnp.bfloat16)
    attended = lax.map(attend_block, (queries.reshape(ROWS // 64, 64, QUERY_HEADS * HEAD_SIZE), cached_key_rows.reshape(ROWS // 64, 64, KVH, CTX, HEAD_SIZE), cached_value_rows.reshape(ROWS // 64, 64, KVH, CTX, HEAD_SIZE), lengths.reshape(ROWS // 64, 64)))
    return (queries, attended.reshape(ROWS, QUERY_HEADS * HEAD_SIZE))
```

```python
import functools
import math

import jax
import jax.numpy as jnp
import numpy as np
from jax import lax
from jax.experimental import pallas as pl
from jax.experimental.pallas import tpu as pltpu
from jax.sharding import PartitionSpec as P

MESH = pl.DeviceIdType.MESH
LANES = 128
SWAPPED = 32


def remote(src, dst, send_sem, recv_sem, axis, peer):
    return pltpu.make_async_remote_copy(
        src_ref=src,
        dst_ref=dst,
        send_sem=send_sem,
        recv_sem=recv_sem,
        device_id={axis: peer},
        device_id_type=MESH,
    )


def greet(counts):
    barrier = pltpu.get_barrier_semaphore()
    total = 0
    for axis, count in counts:
        me = lax.axis_index(axis)
        for d in range(1, count):
            pl.semaphore_signal(
                barrier, inc=1, device_id={axis: lax.rem(me + d, count)}, device_id_type=MESH
            )
            total += 1
    pl.semaphore_wait(barrier, total)


def step_kernel(
    n_ad,
    n_tp,
    cap,
    rank,
    swapped,
    chunk,
    ids_ref,
    table_ref,
    lens_ref,
    lengths_ref,
    tokens_hbm,
    rope_hbm,
    weight_hbm,
    down_hbm,
    up_hbm,
    keys_hbm,
    values_hbm,
    out_hbm,
    att_hbm,
    tokens_ref,
    rope,
    mark,
    unpack,
    cosine,
    sine,
    packed,
    gathered,
    arrived,
    spread,
    outgoing,
    returned,
    part_send,
    part_recv,
    acc,
    weight_buf,
    down_buf,
    up_buf,
    out_ref,
    att_ref,
    heads_f32,
    heads_bf16,
    swap_keys,
    swap_values,
    every,
    keys,
    values,
    part,
    stat,
    part_in,
    stat_in,
    weight_sem,
    load_sem,
    cache_sem,
    done_sem,
    tok_send,
    tok_recv,
    row_send,
    row_recv,
    sum_send,
    sum_recv,
    ret_send,
    ret_recv,
    swap_send,
    swap_recv,
    q_send,
    q_recv,
    p_send,
    p_recv,
    s_send,
    s_recv,
):
    ad = lax.axis_index("ad")
    tp = lax.axis_index("tp")
    rows, features = tokens_ref.shape
    columns = out_ref.shape[1]
    depth = weight_buf.shape[1]
    slots = weight_buf.shape[0]
    subs = features // depth
    steps = n_tp * subs
    per = LANES // rank
    held_here = down_buf.shape[0] // rank
    pairs = down_buf.shape[0] // LANES
    tiles = down_buf.shape[0] // 256
    per_tile = 256 // LANES
    groups = n_ad // 2
    rows2 = 2 * cap
    kv_mine, _, pair_rows, size = heads_bf16.shape
    group = pair_rows // 2
    span = keys_hbm.shape[2]
    width = columns // kv_mine
    spread_rows = rows - swapped
    chunks = spread_rows // chunk
    units = chunk // 2
    context = n_tp * span
    scale = 1.0 / math.sqrt(size)
    f32, bf16 = jnp.float32, jnp.bfloat16

    def weight_copy(i):
        owner = lax.rem(tp + n_tp - i // subs, n_tp)
        start = pl.multiple_of(owner * features + (i % subs) * depth, depth)
        return pltpu.make_async_copy(
            weight_hbm.at[pl.ds(start, depth), :], weight_buf.at[i % slots], weight_sem.at[i % slots]
        )

    tokens_copy = pltpu.make_async_copy(tokens_hbm, tokens_ref, load_sem.at[2])
    rope_copy = pltpu.make_async_copy(rope_hbm, rope, load_sem.at[3])
    down_copy = pltpu.make_async_copy(down_hbm, down_buf, load_sem.at[0])
    up_copy = pltpu.make_async_copy(up_hbm, up_buf, load_sem.at[1])
    tokens_copy.start()
    down_copy.start()
    for i in range(slots):
        weight_copy(i).start()
    rope_copy.start()
    up_copy.start()
    early = pl.ds(0, swapped)
    late = pl.ds(swapped, spread_rows)
    cache_copies = []
    for j in range(kv_mine):
        for which, source, near, far in (
            (0, keys_hbm, swap_keys, keys),
            (1, values_hbm, swap_values, values),
        ):
            cache_copies.append(
                pltpu.make_async_copy(
                    source.at[early, tp * kv_mine + j], near.at[j, :, 0], cache_sem.at[j, which, n_tp]
                )
            )
            for t in range(n_tp):
                cache_copies.append(
                    pltpu.make_async_copy(
                        source.at[late, t * kv_mine + j], far.at[j, :, t], cache_sem.at[j, which, t]
                    )
                )

    greet((("ad", n_ad), ("tp", n_tp)))
    tokens_copy.wait()

    tok_copies = []
    for e in range(1, n_tp):
        copy = remote(
            tokens_ref, gathered.at[e], tok_send.at[e], tok_recv.at[e], "tp", lax.rem(tp + e, n_tp)
        )
        copy.start()
        tok_copies.append(copy)

    index0 = lax.broadcasted_iota(jnp.int32, (rows, rows), 0)
    index1 = lax.broadcasted_iota(jnp.int32, (rows, rows), 1)
    diagonal = index0 == index1

    def to_column(row):
        return jnp.sum(jnp.where(diagonal, row, 0.0), axis=1, keepdims=True)

    def to_row(column):
        return jnp.sum(jnp.where(diagonal, column, 0.0), axis=0, keepdims=True)

    adapters = table_ref.shape[1]
    ids_column = to_column(ids_ref[...].astype(f32))
    adapter = lax.broadcasted_iota(jnp.int32, (rows, adapters), 1).astype(f32)
    slot_column = jnp.sum(
        jnp.where(ids_column == adapter, table_ref[...].astype(f32), 0.0), axis=1, keepdims=True
    )
    owner_column = jnp.floor((slot_column + 0.5) * (1.0 / held_here))
    owner_row = to_row(owner_column)
    same = owner_column == owner_row
    place_column = owner_column * cap + jnp.sum(
        jnp.where(same & (index1 < index0), 1.0, 0.0), axis=1, keepdims=True
    )
    place_row = owner_row * cap + jnp.sum(
        jnp.where(same & (index0 < index1), 1.0, 0.0), axis=0, keepdims=True
    )
    mark[...] = jnp.broadcast_to(slot_column - owner_column * held_here + 1.0, (rows, LANES)).astype(
        bf16
    )
    cell_row = lax.broadcasted_iota(jnp.int32, (cap, rows), 0)

    def pack_into(d, peer, target):
        pick = ((cell_row + peer * cap).astype(f32) == place_row).astype(bf16)

        @pl.loop(0, features // 512)
        def _(c):
            at = pl.ds(pl.multiple_of(c * 512, 512), 512)
            target[d, :, at] = jnp.dot(
                pick, tokens_ref[:, at], preferred_element_type=f32
            ).astype(bf16)

        target[d, :, pl.ds(features, LANES)] = jnp.dot(
            pick, mark[...], preferred_element_type=f32
        ).astype(bf16)

    row_copies = {}
    for d in (4, 3, 5, 2, 6, 1, 7) if n_ad == 8 else range(1, n_ad):
        peer = lax.rem(ad + d, n_ad)
        pack_into(d, peer, packed)
        copy = remote(packed.at[d], arrived.at[d], row_send.at[d], row_recv.at[d], "ad", peer)
        copy.start()
        row_copies[d] = copy
    pack_into(0, ad, arrived)

    cells = lax.broadcasted_iota(jnp.int32, (rows, n_ad * cap), 1).astype(f32)
    unpack[...] = (cells == place_column).astype(bf16)
    moment = to_column(lens_ref[...].astype(f32)) - 1.0
    chosen = (lax.broadcasted_iota(jnp.int32, (rows, context), 1).astype(f32) == moment).astype(bf16)
    rope_copy.wait()
    turn = jnp.dot(chosen, rope[0], preferred_element_type=f32)
    for k in range(1, rope.shape[0]):
        turn = turn + jnp.dot(chosen, rope[k], preferred_element_type=f32)
    cosine[...] = turn[:, :size]
    sine[...] = turn[:, size:]

    swap_copies = []

    def swap(which, source, target):
        for j in range(kv_mine):
            for e in range(1, n_tp):
                peer = lax.rem(tp + e, n_tp)
                copy = remote(
                    source.at[early, peer * kv_mine + j],
                    target.at[j, :, e],
                    swap_send.at[which, j, e],
                    swap_recv.at[which, j, e],
                    "tp",
                    peer,
                )
                copy.start()
                swap_copies.append((j, copy))

    def base_chunk(e):
        if e:
            tok_copies[e - 1].wait_recv()
        block = tokens_ref if e == 0 else gathered.at[e]
        for sub in range(subs):
            i = e * subs + sub
            weight_copy(i).wait()

            @pl.loop(0, columns // 256)
            def _(c):
                at = pl.ds(pl.multiple_of(c * 256, 256), 256)
                product = jnp.dot(
                    block[:, pl.ds(sub * depth, depth)],
                    weight_buf[i % slots, :, at],
                    preferred_element_type=f32,
                )
                if i == 0:
                    acc[:, at] = product
                else:
                    acc[:, at] += product

            if i + slots < steps:
                weight_copy(i + slots).start()

    lane2 = lax.broadcasted_iota(jnp.int32, (rows2, LANES), 1)
    part_of = (lane2 // rank).astype(f32)
    lane1 = lax.broadcasted_iota(jnp.int32, (cap, LANES), 1)
    sum_copies = {}
    ret_copies = []

    def ids_of(g):
        return (
            arrived[pl.ds(2 * g, 2), :, pl.ds(features, LANES)].reshape(rows2, LANES).astype(f32)
            - 1.0
        )

    def shrink(g):
        for d in (2 * g, 2 * g + 1):
            if d:
                row_copies[d].wait_recv()
        if g == 0:
            down_copy.wait()
        ids = ids_of(g) - part_of

        def tile(t, total):
            product = lax.dot_general(
                arrived[pl.ds(2 * g, 2), :, pl.ds(0, features)].reshape(rows2, features),
                down_buf[pl.ds(pl.multiple_of(t * 256, 256), 256), :],
                (((1,), (1,)), ((), ())),
                preferred_element_type=f32,
            )
            for k in range(per_tile):
                want = ((t * per_tile + k) * per).astype(f32)
                total = total + jnp.where(
                    ids == want, product[:, k * LANES : (k + 1) * LANES], 0.0
                )
            return total

        total = lax.fori_loop(0, tiles, tile, jnp.zeros((rows2, LANES), f32))
        total = total + pltpu.roll(total, rank, 1)
        part_send[g] = jnp.where(lane1 < rank, total[:cap], total[cap:])
        for e in range(1, n_tp):
            copy = remote(
                part_send.at[g],
                part_recv.at[g, e],
                sum_send.at[g, e],
                sum_recv.at[g, e],
                "tp",
                lax.rem(tp + e, n_tp),
            )
            copy.start()
            sum_copies[g, e] = copy

    def expand(g, j):
        if j == 0:
            if g == 0:
                up_copy.wait()
            total = part_send[g]
            for e in range(1, n_tp):
                sum_copies[g, e].wait_recv()
                total = total + part_recv[g, e]
            turned = pltpu.roll(total, rank, 1)
            both = jnp.concatenate(
                [jnp.where(lane1 < rank, total, turned), jnp.where(lane1 < rank, turned, total)],
                axis=0,
            )
            ids = ids_of(g) - part_of
            for k in range(pairs):
                spread[g, :, k * LANES : (k + 1) * LANES] = jnp.where(
                    ids == float(k * per), both, 0.0
                ).astype(bf16)

        @pl.loop(0, width // 256)
        def _(c):
            at = pl.ds(pl.multiple_of(c * 256, 256), 256)
            source = pl.ds(pl.multiple_of(j * width + c * 256, 256), 256)
            change = jnp.dot(spread[g], up_buf[:, source], preferred_element_type=f32)
            outgoing[j, pl.ds(2 * g, 2), :, at] = change.astype(bf16).reshape(2, cap, 256)

        for d in (2 * g, 2 * g + 1):
            if d:
                copy = remote(
                    outgoing.at[j, d],
                    returned.at[j, ad],
                    ret_send.at[j, d],
                    ret_recv.at[j, d],
                    "ad",
                    lax.rem(ad + n_ad - d, n_ad),
                )
                copy.start()
                ret_copies.append((j, copy))
            else:
                returned[j, ad] = outgoing[j, 0]

    done_copies = []

    def finish(k, where, source, target):
        copy = pltpu.make_async_copy(source.at[where], target.at[where], done_sem.at[k])
        copy.start()
        done_copies.append(copy)

    sends = {}
    late_pairs = pl.ds(swapped // 2, spread_rows // 2)

    def rotate(j):
        for k, copy in ret_copies:
            if k == j:
                copy.wait_recv()
        for c in range(width // 256):
            at = pl.ds(j * width + c * 256, 256)
            delta = jnp.dot(
                unpack[...],
                returned[j, :, :, pl.ds(c * 256, 256)].reshape(n_ad * cap, 256),
                preferred_element_type=f32,
            )
            query = acc[:, at] + delta
            pieces = []
            for h in range(256 // size):
                one = query[:, h * size : (h + 1) * size]
                piece = one * cosine[...] + pltpu.roll(one, size // 2, 1) * sine[...]
                heads_f32[j, :, c * (256 // size) + h, :] = piece
                pieces.append(piece)
            out_ref[:, at] = jnp.concatenate(pieces, axis=1).astype(bf16)
        heads_bf16[j] = heads_f32[j].reshape(rows // 2, pair_rows, size).astype(bf16)
        for c in range(chunks):
            for e in range(1, n_tp):
                copy = remote(
                    heads_bf16.at[j, pl.ds(swapped // 2 + c * units, units)],
                    every.at[j, pl.ds(c * units, units), tp],
                    q_send.at[j, c, e],
                    q_recv.at[j, c, e],
                    "tp",
                    lax.rem(tp + e, n_tp),
                )
                copy.start()
                sends[j, c, e] = copy
        every[j, :, tp] = heads_bf16[j, late_pairs]
        finish(j, (slice(None), pl.ds(j * width, width)), out_ref, out_hbm)

    lane = lax.broadcasted_iota(jnp.int32, (group, LANES), 1)
    half = LANES // 2

    def flip(x, k):
        return jnp.where((lane // k) % 2 == 1, pltpu.roll(x, k, 1), pltpu.roll(x, LANES - k, 1))

    def settle(j, first, count, k):
        at = pl.ds(first, count)
        for h in range(group):
            att_ref[at, j * width + h * size : j * width + (h + 1) * size] = heads_f32[
                j, at, h, :
            ].astype(bf16)
        finish(k, (at, pl.ds(j * width, width)), att_ref, att_hbm)

    near_place = lax.rem(tp + n_tp - (lane % half) // span, n_tp) * span + lane % span
    far_place = tp * span + lane % span
    seat = lane % span
    seat_of = lane // span
    ones = jnp.ones((LANES, LANES), bf16)
    belongs = (
        lax.broadcasted_iota(jnp.int32, (LANES, LANES), 0) // span
        == lax.broadcasted_iota(jnp.int32, (LANES, LANES), 1) // span
    ).astype(bf16)

    def attend_near(j):
        for k, copy in swap_copies:
            if k == j:
                copy.wait_recv()

        @pl.loop(0, swapped // 8)
        def _(b):
            for u in range(4):
                p = b * 4 + u
                score = lax.dot_general(
                    heads_bf16[j, p],
                    swap_keys[j, pl.ds(2 * p, 2)].reshape(LANES, size),
                    (((1,), (1,)), ((), ())),
                    preferred_element_type=f32,
                )
                score = jnp.where(lane < half, score[:group], score[group:]) * scale
                limit = jnp.where(lane < half, lengths_ref[2 * p], lengths_ref[2 * p + 1])
                valid = near_place < limit
                score = jnp.where(valid, score, -1e30)
                peak = score
                k = half // 2
                while k:
                    peak = jnp.maximum(peak, flip(peak, k))
                    k //= 2
                weight = jnp.where(valid, jnp.exp(score - peak), 0.0)
                weight = jnp.concatenate(
                    [jnp.where(lane < half, weight, 0.0), jnp.where(lane < half, 0.0, weight)], axis=0
                ).astype(bf16)
                total = jnp.dot(weight, ones, preferred_element_type=f32)
                result = jnp.dot(
                    weight,
                    swap_values[j, pl.ds(2 * p, 2)].reshape(LANES, size),
                    preferred_element_type=f32,
                )
                heads_f32[j, pl.ds(2 * p, 2)] = (result / total).reshape(2, group, size)

        settle(j, 0, swapped, kv_mine + j)

    unroll = 4
    outs = []

    def attend(j, c):
        for e in range(1, n_tp):
            sends[j, c, e].wait_recv()

        def some(b, held):
            peaks, totals = held
            for u in range(unroll):
                local = b * unroll + u
                p = c * units + local
                r = pl.multiple_of(2 * p, 2)
                score = lax.dot_general(
                    every[j, p].reshape(n_tp * pair_rows, size),
                    keys[j, pl.ds(r, 2)].reshape(LANES, size),
                    (((1,), (1,)), ((), ())),
                    preferred_element_type=f32,
                )
                merged = score[:group]
                for i in range(2):
                    for t in range(n_tp):
                        at = t * pair_rows + i * group
                        merged = jnp.where(
                            seat_of == i * n_tp + t, score[at : at + group], merged
                        )
                limit = jnp.where(
                    lane < half, lengths_ref[swapped + 2 * p], lengths_ref[swapped + 2 * p + 1]
                )
                valid = far_place < limit
                merged = jnp.where(valid, merged * scale, -1e30)
                peak = merged
                k = span // 2
                while k:
                    peak = jnp.maximum(peak, flip(peak, k))
                    k //= 2
                weight = jnp.where(valid, jnp.exp(merged - peak), 0.0)
                total = jnp.dot(weight.astype(bf16), belongs, preferred_element_type=f32)
                blocks = [
                    jnp.where(seat_of == i * n_tp + t, weight, 0.0)
                    for t in range(n_tp)
                    for i in range(2)
                ]
                result = jnp.dot(
                    jnp.concatenate(blocks, axis=0).astype(bf16),
                    values[j, pl.ds(r, 2)].reshape(LANES, size),
                    preferred_element_type=f32,
                ).astype(bf16)
                for t in range(n_tp):
                    part[j, t, p] = result[t * pair_rows : (t + 1) * pair_rows]
                peaks = jnp.where(seat == local, peak, peaks)
                totals = jnp.where(seat == local, total, totals)
            return peaks, totals

        zero = jnp.zeros((group, LANES), f32)
        peaks, totals = lax.fori_loop(0, units // unroll, some, (zero, zero))
        stat[j, c, 0] = peaks
        stat[j, c, 1] = totals
        at = pl.ds(c * units, units)
        for e in range(1, n_tp):
            peer = lax.rem(tp + e, n_tp)
            s = remote(
                stat.at[j, c], stat_in.at[j, c, e], s_send.at[j, c, e], s_recv.at[j, c, e], "tp", peer
            )
            p = remote(
                part.at[j, peer, at],
                part_in.at[j, e, at],
                p_send.at[j, c, e],
                p_recv.at[j, c, e],
                "tp",
                peer,
            )
            s.start()
            p.start()
            outs.append((j, c, s))
            outs.append((j, c, p))
        part_in[j, 0, at] = part[j, tp, at]
        stat_in[j, c, 0] = stat[j, c]

    def combine(j, c):
        for k, b, copy in outs:
            if (k, b) == (j, c):
                copy.wait_recv()
        peaks = [stat_in[j, c, e, 0] for e in range(n_tp)]
        top = functools.reduce(jnp.maximum, peaks)
        factors = [jnp.exp(s - top) for s in peaks]
        denom = sum(f * stat_in[j, c, e, 1] for e, f in enumerate(factors))
        shares = [f / denom for f in factors]

        @pl.loop(0, units // unroll)
        def _(b):
            for u in range(unroll):
                local = b * unroll + u
                p = c * units + local
                mine = tp * span + local
                result = jnp.zeros((pair_rows, size), f32)
                for e in range(n_tp):
                    share = jnp.concatenate(
                        [
                            jnp.sum(
                                jnp.where(lane == i * half + mine, shares[e], 0.0),
                                axis=1,
                                keepdims=True,
                            )
                            for i in range(2)
                        ],
                        axis=0,
                    )
                    result = result + share * part_in[j, e, p].astype(f32)
                heads_f32[j, pl.ds(swapped + 2 * p, 2)] = result.reshape(2, group, size)

        settle(j, swapped + c * chunk, chunk, 2 * kv_mine + j * chunks + c)

    base_chunk(0)
    shrink(0)
    base_chunk(1)
    base_chunk(2)
    swap(0, keys_hbm, swap_keys)
    base_chunk(3)
    for copy in cache_copies:
        copy.start()
    for g in range(1, groups):
        shrink(g)
    for g in range(groups):
        expand(g, 0)
    for g in range(groups):
        expand(g, 1)
    swap(1, values_hbm, swap_values)
    rotate(0)
    for copy in cache_copies:
        copy.wait()
    for c in range(chunks - 1):
        attend(0, c)
    rotate(1)
    attend(0, chunks - 1)
    attend_near(0)
    attend_near(1)
    for c in range(chunks):
        attend(1, c)
        combine(0, c)
    for c in range(chunks):
        combine(1, c)

    for copy in list(row_copies.values()) + tok_copies + list(sum_copies.values()):
        copy.wait_send()
    for _, copy in ret_copies + swap_copies:
        copy.wait_send()
    for copy in list(sends.values()) + [copy for _, _, copy in outs]:
        copy.wait_send()
    for copy in done_copies:
        copy.wait()


def rope_table(context, head_dim):
    half = head_dim // 2
    freq = np.exp(np.arange(half, dtype=np.float64) * (-2.0 * math.log(500000.0) / head_dim))
    freq = freq.astype(np.float32).astype(np.float64)
    angle = (np.arange(context, dtype=np.float64)[:, None] * freq[None, :]).astype(np.float32)
    cosine, sine = np.cos(angle.astype(np.float64)), np.sin(angle.astype(np.float64))
    rest = np.concatenate([cosine, cosine, -sine, sine], axis=1).astype(np.float32)
    terms = []
    for _ in range(3):
        term = rest.astype(jnp.bfloat16)
        terms.append(term)
        rest = rest - term.astype(np.float32)
    return np.stack(terms)


def fused_device(
    tokens,
    query_weight,
    adapter_down_weight,
    adapter_up_weight,
    row_adapter_index,
    adapter_table_slot,
    lengths,
    cached_key_rows,
    cached_value_rows,
):
    rows, features = tokens.shape
    columns = query_weight.shape[1]
    n_ad = lax.axis_size("ad")
    n_tp = lax.axis_size("tp")
    held = adapter_down_weight.shape[0]
    rank = adapter_down_weight.shape[2]
    _, kv_heads, span, head_dim = cached_key_rows.shape
    cap = -(-(384 // n_ad) // 16) * 16

    depth = 1024
    slot_count = 4
    swapped = SWAPPED
    chunk = 32
    heads = columns // head_dim
    spread_rows = rows - swapped
    chunks = spread_rows // chunk
    kv_mine = kv_heads // n_tp
    group = heads // kv_mine
    pairs = rows // 2
    spread_pairs = spread_rows // 2
    width = columns // kv_mine
    vmem = pl.BlockSpec(memory_space=pltpu.VMEM)
    smem = pl.BlockSpec(memory_space=pltpu.SMEM)
    anywhere = pl.BlockSpec(memory_space=pl.ANY)
    bf16, f32 = jnp.bfloat16, jnp.float32
    dma = pltpu.SemaphoreType.DMA
    groups = n_ad // 2
    rope = rope_table(n_tp * span, head_dim)
    return pl.pallas_call(
        functools.partial(step_kernel, n_ad, n_tp, cap, rank, swapped, chunk),
        out_shape=(jax.ShapeDtypeStruct((rows, columns), bf16),) * 2,
        in_specs=[vmem] * 3 + [smem] + [anywhere] * 7,
        out_specs=(anywhere, anywhere),
        scratch_shapes=[
            pltpu.VMEM((rows, features), bf16),
            pltpu.VMEM(rope.shape, bf16),
            pltpu.VMEM((rows, LANES), bf16),
            pltpu.VMEM((rows, n_ad * cap), bf16),
            pltpu.VMEM((rows, head_dim), f32),
            pltpu.VMEM((rows, head_dim), f32),
            pltpu.VMEM((n_ad, cap, features + LANES), bf16),
            pltpu.VMEM((n_tp, rows, features), bf16),
            pltpu.VMEM((n_ad, cap, features + LANES), bf16),
            pltpu.VMEM((groups, 2 * cap, held * rank), bf16),
            pltpu.VMEM((kv_mine, n_ad, cap, width), bf16),
            pltpu.VMEM((kv_mine, n_ad, cap, width), bf16),
            pltpu.VMEM((groups, cap, LANES), f32),
            pltpu.VMEM((groups, n_tp, cap, LANES), f32),
            pltpu.VMEM((rows, columns), f32),
            pltpu.VMEM((slot_count, depth, columns), bf16),
            pltpu.VMEM((held * rank, features), bf16),
            pltpu.VMEM((held * rank, columns), bf16),
            pltpu.VMEM((rows, columns), bf16),
            pltpu.VMEM((rows, columns), bf16),
            pltpu.VMEM((kv_mine, rows, group, head_dim), f32),
            pltpu.VMEM((kv_mine, pairs, 2 * group, head_dim), bf16),
            pltpu.VMEM((kv_mine, swapped, n_tp, span, head_dim), bf16),
            pltpu.VMEM((kv_mine, swapped, n_tp, span, head_dim), bf16),
            pltpu.VMEM((kv_mine, spread_pairs, n_tp, 2 * group, head_dim), bf16),
            pltpu.VMEM((kv_mine, spread_rows, n_tp, span, head_dim), bf16),
            pltpu.VMEM((kv_mine, spread_rows, n_tp, span, head_dim), bf16),
            pltpu.VMEM((kv_mine, n_tp, spread_pairs, 2 * group, head_dim), bf16),
            pltpu.VMEM((kv_mine, chunks, 2, group, LANES), f32),
            pltpu.VMEM((kv_mine, n_tp, spread_pairs, 2 * group, head_dim), bf16),
            pltpu.VMEM((kv_mine, chunks, n_tp, 2, group, LANES), f32),
            dma((slot_count,)),
            dma((4,)),
            dma((kv_mine, 2, n_tp + 1)),
            dma((2 * kv_mine + kv_mine * chunks,)),
            dma((n_tp,)),
            dma((n_tp,)),
            dma((n_ad,)),
            dma((n_ad,)),
            dma((groups, n_tp)),
            dma((groups, n_tp)),
            dma((kv_mine, n_ad)),
            dma((kv_mine, n_ad)),
            dma((2, kv_mine, n_tp)),
            dma((2, kv_mine, n_tp)),
            dma((kv_mine, chunks, n_tp)),
            dma((kv_mine, chunks, n_tp)),
            dma((kv_mine, chunks, n_tp)),
            dma((kv_mine, chunks, n_tp)),
            dma((kv_mine, chunks, n_tp)),
            dma((kv_mine, chunks, n_tp)),
        ],
        compiler_params=pltpu.CompilerParams(
            collective_id=0, has_side_effects=True, vmem_limit_bytes=60 * 1024 * 1024
        ),
        name="step",
    )(
        row_adapter_index[None, :],
        adapter_table_slot[None, :],
        lengths[None, :],
        lengths,
        tokens,
        jnp.asarray(rope),
        query_weight,
        adapter_down_weight.transpose(0, 2, 1).reshape(held * rank, features),
        adapter_up_weight.reshape(held * rank, columns),
        cached_key_rows,
        cached_value_rows,
    )


def rotate(query, lengths):
    head_dim = query.shape[-1]
    half = head_dim // 2
    freq = jnp.exp(jnp.arange(half, dtype=jnp.float32) * (-2.0 * math.log(500000.0) / head_dim))
    angle = (lengths - 1).astype(jnp.float32)[:, None, None] * freq[None, None, :]
    cosine = jnp.cos(angle)
    sine = jnp.sin(angle)
    first = query[..., :half]
    second = query[..., half:]
    return jnp.concatenate(
        [first * cosine - second * sine, second * cosine + first * sine], axis=-1
    )


def lookup(ids, adapter_table_slot):
    table = jnp.arange(adapter_table_slot.shape[0], dtype=jnp.int32)
    return jnp.sum(
        jnp.where(ids[:, None] == table[None, :], adapter_table_slot[None, :], 0), axis=1
    )


def shrink_rows(input_rows, local_partial, adapter_down_weight):
    adapter_row_count = adapter_down_weight.shape[0]
    select_rows = (
        local_partial[:, None] == jnp.arange(adapter_row_count, dtype=jnp.int32)[None, :]
    ).astype(jnp.float32)
    update_terms = jnp.einsum(
        "nt,vtm->nvm", input_rows, adapter_down_weight, preferred_element_type=jnp.float32
    )
    return (select_rows, jnp.sum(update_terms * select_rows[:, :, None], axis=1))


def expand_rows(select_rows, reduced_rows, adapter_up_weight):
    spread_rows = (select_rows[:, :, None] * reduced_rows.astype(jnp.float32)[:, None, :]).astype(
        jnp.bfloat16
    )
    return jnp.einsum(
        "pow,owu->pu", spread_rows, adapter_up_weight, preferred_element_type=jnp.float32
    ).astype(jnp.bfloat16)


def per_device(
    tokens,
    query_weight,
    adapter_down_weight,
    adapter_up_weight,
    row_adapter_index,
    adapter_table_slot,
    lengths,
    cached_key_rows,
    cached_value_rows,
):
    rows = tokens.shape[0]
    columns = query_weight.shape[1]
    tp_count = lax.axis_size("tp")
    owner_partials = adapter_down_weight.shape[0]
    base = jnp.dot(
        lax.all_gather(tokens, "tp", axis=1, tiled=True),
        query_weight,
        preferred_element_type=jnp.float32,
    )
    combined_output, every_id = (
        lax.all_gather(tokens, "ad", axis=0, tiled=True),
        lax.all_gather(row_adapter_index, "ad", axis=0, tiled=True),
    )
    slots = lookup(every_id, adapter_table_slot)
    mine = slots // owner_partials == lax.axis_index("ad")
    local_partial = jnp.where(mine, slots % owner_partials, -1)
    select_rows, partial_value_sum = shrink_rows(
        combined_output, local_partial, adapter_down_weight
    )
    reduced_rows = lax.psum(partial_value_sum, "tp").astype(jnp.bfloat16)
    lowrank_change = expand_rows(select_rows, reduced_rows, adapter_up_weight)
    delta = lax.psum_scatter(
        lowrank_change.astype(jnp.float32).astype(jnp.bfloat16),
        "ad",
        scatter_dimension=0,
        tiled=True,
    ).astype(jnp.float32)
    head_dim = cached_key_rows.shape[3]
    query = (base + delta).reshape(rows, columns // head_dim, head_dim)
    queries = rotate(query, lengths).reshape(rows, columns).astype(jnp.bfloat16)
    every_head = lax.all_gather(queries, "tp", axis=1, tiled=True)
    kv_heads = cached_key_rows.shape[1]
    span = cached_key_rows.shape[2]
    grouped = every_head.reshape(rows, kv_heads, -1, head_dim)
    scores = jnp.einsum(
        "rkgd,rkpd->rkgp", grouped, cached_key_rows, preferred_element_type=jnp.float32
    ) * (1.0 / math.sqrt(head_dim))
    position = lax.axis_index("tp") * span + jnp.arange(span, dtype=jnp.int32)
    valid = (position[None, :] < lengths[:, None])[:, None, None, :]
    scores = jnp.where(valid, scores, -1e30)
    peak = jnp.max(scores, axis=-1)
    weights = jnp.where(valid, jnp.exp(scores - peak[..., None]), 0.0)
    total = jnp.sum(weights, axis=-1)
    partial_out = jnp.einsum(
        "rkgp,rkpd->rkgd",
        weights.astype(jnp.bfloat16),
        cached_value_rows,
        preferred_element_type=jnp.float32,
    ).astype(jnp.bfloat16)
    peaks, totals = (
        lax.all_to_all(
            peak.reshape(rows, tp_count, -1), "tp", split_axis=1, concat_axis=1, tiled=True
        ),
        lax.all_to_all(
            total.reshape(rows, tp_count, -1), "tp", split_axis=1, concat_axis=1, tiled=True
        ),
    )
    partials = lax.all_to_all(
        partial_out.reshape(rows, tp_count, -1), "tp", split_axis=1, concat_axis=1, tiled=True
    )
    highest = jnp.max(peaks, axis=1, keepdims=True)
    factor = jnp.exp(peaks - highest)
    numer = jnp.sum(
        factor[..., None] * partials.reshape(rows, tp_count, -1, head_dim).astype(jnp.float32),
        axis=1,
    )
    denom = jnp.sum(factor * totals, axis=1)
    attended = (numer / denom[..., None]).reshape(rows, columns).astype(jnp.bfloat16)
    return (queries, attended)


def solution(mesh):
    fits = mesh.shape["tp"] == 4 and mesh.shape["ad"] == 8
    return jax.shard_map(
        fused_device if fits else per_device,
        mesh=mesh,
        in_specs=(
            P("ad", "tp"),
            P(None, "tp"),
            P("ad", "tp", None),
            P("ad", None, "tp"),
            P("ad"),
            P(),
            P("ad"),
            P("ad", None, "tp", None),
            P("ad", None, "tp", None),
        ),
        out_specs=(P("ad", "tp"), P("ad", "tp")),
        check_vma=False,
    )
```

```python
import functools
import math

import jax
import jax.numpy as jnp
import numpy as np
from jax import lax
from jax.experimental import pallas as pl
from jax.experimental.pallas import tpu as pltpu
from jax.sharding import PartitionSpec as P

MESH = pl.DeviceIdType.MESH
LANES = 128
SWAPPED = 64
CHUNK = 32


def remote(src, dst, send_sem, recv_sem, axis, peer):
    return pltpu.make_async_remote_copy(
        src_ref=src,
        dst_ref=dst,
        send_sem=send_sem,
        recv_sem=recv_sem,
        device_id={axis: peer},
        device_id_type=MESH,
    )


def greet(counts):
    barrier = pltpu.get_barrier_semaphore()
    total = 0
    for axis, count in counts:
        me = lax.axis_index(axis)
        for d in range(1, count):
            pl.semaphore_signal(
                barrier, inc=1, device_id={axis: lax.rem(me + d, count)}, device_id_type=MESH
            )
            total += 1
    pl.semaphore_wait(barrier, total)


def step_kernel(
    n_ad,
    n_tp,
    cap,
    rank,
    swapped,
    chunk,
    ids_ref,
    table_ref,
    lens_ref,
    lengths_ref,
    tokens_hbm,
    rope_hbm,
    weight_hbm,
    down_hbm,
    up_hbm,
    keys_hbm,
    values_hbm,
    out_hbm,
    att_hbm,
    tokens_ref,
    rope,
    mark,
    unpack,
    cosine,
    sine,
    packed,
    gathered,
    arrived,
    spread,
    outgoing,
    returned,
    part_send,
    part_recv,
    acc,
    weight_buf,
    down_buf,
    up_buf,
    out_ref,
    att_ref,
    heads_f32,
    heads_bf16,
    swap_keys,
    swap_values,
    every,
    keys,
    values,
    part,
    stat,
    part_in,
    stat_in,
    weight_sem,
    load_sem,
    cache_sem,
    done_sem,
    tok_send,
    tok_recv,
    row_send,
    row_recv,
    sum_send,
    sum_recv,
    ret_send,
    ret_recv,
    swap_send,
    swap_recv,
    q_send,
    q_recv,
    p_send,
    p_recv,
    s_send,
    s_recv,
):
    ad = lax.axis_index("ad")
    tp = lax.axis_index("tp")
    rows, features = tokens_ref.shape
    columns = out_ref.shape[1]
    depth = weight_buf.shape[1]
    slots = weight_buf.shape[0]
    subs = features // depth
    steps = n_tp * subs
    per = LANES // rank
    held_here = down_buf.shape[0] // rank
    pairs = down_buf.shape[0] // LANES
    tiles = down_buf.shape[0] // 256
    per_tile = 256 // LANES
    groups = n_ad // 2
    rows2 = 2 * cap
    kv_mine, _, pair_rows, size = heads_bf16.shape
    group = pair_rows // 2
    span = keys_hbm.shape[2]
    width = columns // kv_mine
    spread_rows = rows - swapped
    chunks = spread_rows // chunk
    units = chunk // 2
    context = n_tp * span
    scale = 1.0 / math.sqrt(size)
    f32, bf16 = jnp.float32, jnp.bfloat16

    def weight_copy(i):
        owner = lax.rem(tp + n_tp - i // subs, n_tp)
        start = pl.multiple_of(owner * features + (i % subs) * depth, depth)
        return pltpu.make_async_copy(
            weight_hbm.at[pl.ds(start, depth), :], weight_buf.at[i % slots], weight_sem.at[i % slots]
        )

    tokens_copy = pltpu.make_async_copy(tokens_hbm, tokens_ref, load_sem.at[2])
    rope_copy = pltpu.make_async_copy(rope_hbm, rope, load_sem.at[3])
    down_copy = pltpu.make_async_copy(down_hbm, down_buf, load_sem.at[0])
    up_copy = pltpu.make_async_copy(up_hbm, up_buf, load_sem.at[1])
    tokens_copy.start()
    down_copy.start()
    for i in range(slots):
        weight_copy(i).start()
    rope_copy.start()
    up_copy.start()
    early = pl.ds(0, swapped)
    late = pl.ds(swapped, spread_rows)
    cache_copies = []
    for j in range(kv_mine):
        for which, source, near, far in (
            (0, keys_hbm, swap_keys, keys),
            (1, values_hbm, swap_values, values),
        ):
            cache_copies.append(
                pltpu.make_async_copy(
                    source.at[early, tp * kv_mine + j], near.at[j, :, 0], cache_sem.at[j, which, n_tp]
                )
            )
            for t in range(n_tp):
                cache_copies.append(
                    pltpu.make_async_copy(
                        source.at[late, t * kv_mine + j], far.at[j, :, t], cache_sem.at[j, which, t]
                    )
                )

    greet((("ad", n_ad), ("tp", n_tp)))
    tokens_copy.wait()

    tok_copies = []
    for e in range(1, n_tp):
        copy = remote(
            tokens_ref, gathered.at[e], tok_send.at[e], tok_recv.at[e], "tp", lax.rem(tp + e, n_tp)
        )
        copy.start()
        tok_copies.append(copy)

    index0 = lax.broadcasted_iota(jnp.int32, (rows, rows), 0)
    index1 = lax.broadcasted_iota(jnp.int32, (rows, rows), 1)
    diagonal = index0 == index1

    def to_column(row):
        return jnp.sum(jnp.where(diagonal, row, 0.0), axis=1, keepdims=True)

    def to_row(column):
        return jnp.sum(jnp.where(diagonal, column, 0.0), axis=0, keepdims=True)

    adapters = table_ref.shape[1]
    ids_column = to_column(ids_ref[...].astype(f32))
    adapter = lax.broadcasted_iota(jnp.int32, (rows, adapters), 1).astype(f32)
    slot_column = jnp.sum(
        jnp.where(ids_column == adapter, table_ref[...].astype(f32), 0.0), axis=1, keepdims=True
    )
    owner_column = jnp.floor((slot_column + 0.5) * (1.0 / held_here))
    owner_row = to_row(owner_column)
    same = owner_column == owner_row
    place_column = owner_column * cap + jnp.sum(
        jnp.where(same & (index1 < index0), 1.0, 0.0), axis=1, keepdims=True
    )
    place_row = owner_row * cap + jnp.sum(
        jnp.where(same & (index0 < index1), 1.0, 0.0), axis=0, keepdims=True
    )
    mark[...] = jnp.broadcast_to(slot_column - owner_column * held_here + 1.0, (rows, LANES)).astype(
        bf16
    )
    cell_row = lax.broadcasted_iota(jnp.int32, (cap, rows), 0)

    def pack_into(d, peer, target):
        pick = ((cell_row + peer * cap).astype(f32) == place_row).astype(bf16)

        @pl.loop(0, features // 512)
        def _(c):
            at = pl.ds(pl.multiple_of(c * 512, 512), 512)
            target[d, :, at] = jnp.dot(
                pick, tokens_ref[:, at], preferred_element_type=f32
            ).astype(bf16)

        target[d, :, pl.ds(features, LANES)] = jnp.dot(
            pick, mark[...], preferred_element_type=f32
        ).astype(bf16)

    row_copies = {}
    for d in (4, 3, 5, 2, 6, 1, 7) if n_ad == 8 else range(1, n_ad):
        peer = lax.rem(ad + d, n_ad)
        pack_into(d, peer, packed)
        copy = remote(packed.at[d], arrived.at[d], row_send.at[d], row_recv.at[d], "ad", peer)
        copy.start()
        row_copies[d] = copy
    pack_into(0, ad, arrived)

    cells = lax.broadcasted_iota(jnp.int32, (rows, n_ad * cap), 1).astype(f32)
    unpack[...] = (cells == place_column).astype(bf16)
    moment = to_column(lens_ref[...].astype(f32)) - 1.0
    chosen = (lax.broadcasted_iota(jnp.int32, (rows, context), 1).astype(f32) == moment).astype(bf16)
    rope_copy.wait()
    turn = jnp.dot(chosen, rope[0], preferred_element_type=f32)
    for k in range(1, rope.shape[0]):
        turn = turn + jnp.dot(chosen, rope[k], preferred_element_type=f32)
    cosine[...] = turn[:, :size]
    sine[...] = turn[:, size:]

    swap_copies = []

    def swap(which, source, target):
        for j in range(kv_mine):
            for e in range(1, n_tp):
                peer = lax.rem(tp + e, n_tp)
                copy = remote(
                    source.at[early, peer * kv_mine + j],
                    target.at[j, :, e],
                    swap_send.at[which, j, e],
                    swap_recv.at[which, j, e],
                    "tp",
                    peer,
                )
                copy.start()
                swap_copies.append((j, copy))

    def base_chunk(e):
        if e:
            tok_copies[e - 1].wait_recv()
        block = tokens_ref if e == 0 else gathered.at[e]
        for sub in range(subs):
            i = e * subs + sub
            weight_copy(i).wait()

            @pl.loop(0, columns // 256)
            def _(c):
                at = pl.ds(pl.multiple_of(c * 256, 256), 256)
                product = jnp.dot(
                    block[:, pl.ds(sub * depth, depth)],
                    weight_buf[i % slots, :, at],
                    preferred_element_type=f32,
                )
                if i == 0:
                    acc[:, at] = product
                else:
                    acc[:, at] += product

            if i + slots < steps:
                weight_copy(i + slots).start()

    lane2 = lax.broadcasted_iota(jnp.int32, (rows2, LANES), 1)
    part_of = (lane2 // rank).astype(f32)
    lane1 = lax.broadcasted_iota(jnp.int32, (cap, LANES), 1)
    sum_copies = {}
    ret_copies = {}

    def ids_of(g):
        return (
            arrived[pl.ds(2 * g, 2), :, pl.ds(features, LANES)].reshape(rows2, LANES).astype(f32)
            - 1.0
        )

    def shrink(g):
        for d in (2 * g, 2 * g + 1):
            if d:
                row_copies[d].wait_recv()
        if g == 0:
            down_copy.wait()
        ids = ids_of(g) - part_of

        def tile(t, total):
            product = lax.dot_general(
                arrived[pl.ds(2 * g, 2), :, pl.ds(0, features)].reshape(rows2, features),
                down_buf[pl.ds(pl.multiple_of(t * 256, 256), 256), :],
                (((1,), (1,)), ((), ())),
                preferred_element_type=f32,
            )
            for k in range(per_tile):
                want = ((t * per_tile + k) * per).astype(f32)
                total = total + jnp.where(
                    ids == want, product[:, k * LANES : (k + 1) * LANES], 0.0
                )
            return total

        total = lax.fori_loop(0, tiles, tile, jnp.zeros((rows2, LANES), f32))
        total = total + pltpu.roll(total, rank, 1)
        part_send[g] = jnp.where(lane1 < rank, total[:cap], total[cap:])
        for e in range(1, n_tp):
            copy = remote(
                part_send.at[g],
                part_recv.at[g, e],
                sum_send.at[g, e],
                sum_recv.at[g, e],
                "tp",
                lax.rem(tp + e, n_tp),
            )
            copy.start()
            sum_copies[g, e] = copy

    def expand(g, j):
        if j == 0:
            if g == 0:
                up_copy.wait()
            total = part_send[g]
            for e in range(1, n_tp):
                sum_copies[g, e].wait_recv()
                total = total + part_recv[g, e]
            turned = pltpu.roll(total, rank, 1)
            both = jnp.concatenate(
                [jnp.where(lane1 < rank, total, turned), jnp.where(lane1 < rank, turned, total)],
                axis=0,
            )
            ids = ids_of(g) - part_of
            for k in range(pairs):
                spread[g, :, k * LANES : (k + 1) * LANES] = jnp.where(
                    ids == float(k * per), both, 0.0
                ).astype(bf16)

        @pl.loop(0, width // 256)
        def _(c):
            at = pl.ds(pl.multiple_of(c * 256, 256), 256)
            source = pl.ds(pl.multiple_of(j * width + c * 256, 256), 256)
            change = jnp.dot(spread[g], up_buf[:, source], preferred_element_type=f32)
            outgoing[j, pl.ds(2 * g, 2), :, at] = change.astype(bf16).reshape(2, cap, 256)

        for d in (2 * g, 2 * g + 1):
            if d:
                copy = remote(
                    outgoing.at[j, d],
                    returned.at[j, ad],
                    ret_send.at[j, d],
                    ret_recv.at[j, d],
                    "ad",
                    lax.rem(ad + n_ad - d, n_ad),
                )
                if j == 0:
                    copy.start()
                ret_copies[j, d] = copy
            else:
                returned[j, ad] = outgoing[j, 0]

    done_copies = []

    def finish(k, where, source, target):
        copy = pltpu.make_async_copy(source.at[where], target.at[where], done_sem.at[k])
        copy.start()
        done_copies.append(copy)

    sends = {}
    late_pairs = pl.ds(swapped // 2, spread_rows // 2)

    def rotate(j):
        for d in range(1, n_ad):
            ret_copies[j, d].wait_recv()
        for c in range(width // 256):
            at = pl.ds(j * width + c * 256, 256)
            delta = jnp.dot(
                unpack[...],
                returned[j, :, :, pl.ds(c * 256, 256)].reshape(n_ad * cap, 256),
                preferred_element_type=f32,
            )
            query = acc[:, at] + delta
            pieces = []
            for h in range(256 // size):
                one = query[:, h * size : (h + 1) * size]
                piece = one * cosine[...] + pltpu.roll(one, size // 2, 1) * sine[...]
                heads_f32[j, :, c * (256 // size) + h, :] = piece
                pieces.append(piece)
            out_ref[:, at] = jnp.concatenate(pieces, axis=1).astype(bf16)
        heads_bf16[j] = heads_f32[j].reshape(rows // 2, pair_rows, size).astype(bf16)
        for c in range(chunks):
            for e in range(1, n_tp):
                copy = remote(
                    heads_bf16.at[j, pl.ds(swapped // 2 + c * units, units)],
                    every.at[j, tp, pl.ds(c * units, units)],
                    q_send.at[j, c, e],
                    q_recv.at[j, c, e],
                    "tp",
                    lax.rem(tp + e, n_tp),
                )
                copy.start()
                sends[j, c, e] = copy
        every[j, tp] = heads_bf16[j, late_pairs]
        finish(j, (slice(None), pl.ds(j * width, width)), out_ref, out_hbm)

    lane = lax.broadcasted_iota(jnp.int32, (group, LANES), 1)
    half = LANES // 2

    def top_of(x, extent):
        k = extent // 2
        while k:
            flat = x.reshape(-1, LANES)
            up = pltpu.roll(flat, k, 1).reshape(x.shape)
            down = pltpu.roll(flat, LANES - k, 1).reshape(x.shape)
            x = jnp.maximum(x, jnp.where((lane // k) % 2 == 1, up, down))
            k //= 2
        return x

    def settle(j, first, count, k):
        at = pl.ds(first, count)
        for h in range(group):
            att_ref[at, j * width + h * size : j * width + (h + 1) * size] = heads_f32[
                j, at, h, :
            ].astype(bf16)
        finish(k, (at, pl.ds(j * width, width)), att_ref, att_hbm)

    near_place = lax.rem(tp + n_tp - (lane % half) // span, n_tp) * span + lane % span
    far_place = tp * span + lane % span
    seat = lane % span
    seat_of = lane // span
    ones = jnp.ones((LANES, LANES), bf16)
    belongs = (
        lax.broadcasted_iota(jnp.int32, (LANES, LANES), 0) // span
        == lax.broadcasted_iota(jnp.int32, (LANES, LANES), 1) // span
    ).astype(bf16)

    def attend_near(j):
        for k, copy in swap_copies:
            if k == j:
                copy.wait_recv()

        batch = 8

        @pl.loop(0, swapped // (2 * batch))
        def _(b):
            merged, limits = [], []
            for u in range(batch):
                p = b * batch + u
                score = lax.dot_general(
                    heads_bf16[j, p],
                    swap_keys[j, pl.ds(2 * p, 2)].reshape(LANES, size),
                    (((1,), (1,)), ((), ())),
                    preferred_element_type=f32,
                )
                merged.append(jnp.where(lane < half, score[:group], score[group:]))
                limits.append(
                    jnp.where(lane < half, lengths_ref[2 * p], lengths_ref[2 * p + 1])
                )
            valid = near_place[None] < jnp.stack(limits)
            score = jnp.where(valid, jnp.stack(merged) * scale, -1e30)
            peak = top_of(score, half)
            weight = jnp.where(valid, jnp.exp(score - peak), 0.0)
            first = jnp.where(lane < half, weight, 0.0)
            both = jnp.concatenate([first, weight - first], axis=1).astype(bf16)
            total = jnp.dot(
                both.reshape(batch * pair_rows, LANES), ones, preferred_element_type=f32
            )
            for u in range(batch):
                p = b * batch + u
                result = jnp.dot(
                    both[u],
                    swap_values[j, pl.ds(2 * p, 2)].reshape(LANES, size),
                    preferred_element_type=f32,
                )
                result = result / total[u * pair_rows : (u + 1) * pair_rows]
                heads_f32[j, pl.ds(2 * p, 2)] = result.reshape(2, group, size)

        settle(j, 0, swapped, kv_mine + j)

    unroll = 8
    outs = []

    def attend(j, c):
        for e in range(1, n_tp):
            sends[j, c, e].wait_recv()

        def some(b, held):
            peaks, totals = held
            merged, limits = [], []
            for u in range(unroll):
                p = c * units + b * unroll + u
                score = lax.dot_general(
                    jnp.concatenate([every[j, t, p] for t in range(n_tp)], axis=0),
                    keys[j, pl.ds(2 * p, 2)].reshape(LANES, size),
                    (((1,), (1,)), ((), ())),
                    preferred_element_type=f32,
                )
                one = score[:group]
                for i in range(2):
                    for t in range(n_tp):
                        at = t * pair_rows + i * group
                        one = jnp.where(seat_of == i * n_tp + t, score[at : at + group], one)
                merged.append(one)
                limits.append(
                    jnp.where(
                        lane < half, lengths_ref[swapped + 2 * p], lengths_ref[swapped + 2 * p + 1]
                    )
                )
            valid = far_place[None] < jnp.stack(limits)
            score = jnp.where(valid, jnp.stack(merged) * scale, -1e30)
            peak = top_of(score, span)
            weight = jnp.where(valid, jnp.exp(score - peak), 0.0)
            total = jnp.dot(
                weight.reshape(unroll * group, LANES).astype(bf16),
                belongs,
                preferred_element_type=f32,
            )
            for u in range(unroll):
                local = b * unroll + u
                p = c * units + local
                blocks = [
                    jnp.where(seat_of == i * n_tp + t, weight[u], 0.0)
                    for t in range(n_tp)
                    for i in range(2)
                ]
                result = jnp.dot(
                    jnp.concatenate(blocks, axis=0).astype(bf16),
                    values[j, pl.ds(2 * p, 2)].reshape(LANES, size),
                    preferred_element_type=f32,
                ).astype(bf16)
                for t in range(n_tp):
                    part[j, t, p] = result[t * pair_rows : (t + 1) * pair_rows]
                peaks = jnp.where(seat == local, peak[u], peaks)
                totals = jnp.where(seat == local, total[u * group : (u + 1) * group], totals)
            return peaks, totals

        zero = jnp.zeros((group, LANES), f32)
        peaks, totals = lax.fori_loop(0, units // unroll, some, (zero, zero))
        stat[j, c, 0] = peaks
        stat[j, c, 1] = totals
        at = pl.ds(c * units, units)
        for e in range(1, n_tp):
            peer = lax.rem(tp + e, n_tp)
            s = remote(
                stat.at[j, c], stat_in.at[j, c, e], s_send.at[j, c, e], s_recv.at[j, c, e], "tp", peer
            )
            p = remote(
                part.at[j, peer, at],
                part_in.at[j, e, at],
                p_send.at[j, c, e],
                p_recv.at[j, c, e],
                "tp",
                peer,
            )
            s.start()
            p.start()
            outs.append((j, c, s))
            outs.append((j, c, p))
        part_in[j, 0, at] = part[j, tp, at]
        stat_in[j, c, 0] = stat[j, c]

    def combine(j, c):
        for k, b, copy in outs:
            if (k, b) == (j, c):
                copy.wait_recv()
        peaks = [stat_in[j, c, e, 0] for e in range(n_tp)]
        top = functools.reduce(jnp.maximum, peaks)
        factors = [jnp.exp(s - top) for s in peaks]
        denom = sum(f * stat_in[j, c, e, 1] for e, f in enumerate(factors))
        shares = [f / denom for f in factors]

        @pl.loop(0, units // unroll)
        def _(b):
            for u in range(unroll):
                local = b * unroll + u
                p = c * units + local
                mine = tp * span + local
                result = jnp.zeros((pair_rows, size), f32)
                for e in range(n_tp):
                    share = jnp.concatenate(
                        [
                            jnp.sum(
                                jnp.where(lane == i * half + mine, shares[e], 0.0),
                                axis=1,
                                keepdims=True,
                            )
                            for i in range(2)
                        ],
                        axis=0,
                    )
                    result = result + share * part_in[j, e, p].astype(f32)
                heads_f32[j, pl.ds(swapped + 2 * p, 2)] = result.reshape(2, group, size)

        settle(j, swapped + c * chunk, chunk, 2 * kv_mine + j * chunks + c)

    base_chunk(0)
    shrink(0)
    base_chunk(1)
    base_chunk(2)
    swap(0, keys_hbm, swap_keys)
    base_chunk(3)
    for copy in cache_copies:
        copy.start()
    for g in range(1, groups):
        shrink(g)
    swap(1, values_hbm, swap_values)
    for j in range(kv_mine):
        for g in range(groups):
            expand(g, j)
    for j in range(1, kv_mine):
        for d in sorted(range(1, n_ad), key=lambda d: abs(d - n_ad // 2), reverse=True):
            ret_copies[j - 1, d].wait_send()
            ret_copies[j, d].start()
    for copy in cache_copies:
        copy.wait()
    rotate(0)
    attend_near(0)
    for c in range(chunks):
        attend(0, c)
    rotate(1)
    attend_near(1)
    for c in range(chunks):
        combine(0, c)
    for c in range(chunks):
        attend(1, c)
    for c in range(chunks):
        combine(1, c)

    for copy in list(row_copies.values()) + tok_copies + list(sum_copies.values()):
        copy.wait_send()
    for d in range(1, n_ad):
        ret_copies[kv_mine - 1, d].wait_send()
    for _, copy in swap_copies:
        copy.wait_send()
    for copy in list(sends.values()) + [copy for _, _, copy in outs]:
        copy.wait_send()
    for copy in done_copies:
        copy.wait()


def hand_over(first_hbm, second_hbm, out_hbm, att_hbm, held, sem):
    loads = []
    for k, source in enumerate((first_hbm, second_hbm)):
        copy = pltpu.make_async_copy(source, held.at[k], sem.at[0, k])
        copy.start()
        loads.append(copy)
    stores = []
    for k, target in enumerate((out_hbm, att_hbm)):
        loads[k].wait()
        copy = pltpu.make_async_copy(held.at[k], target, sem.at[1, k])
        copy.start()
        stores.append(copy)
    for copy in stores:
        copy.wait()


def rope_table(context, head_dim):
    half = head_dim // 2
    freq = np.exp(np.arange(half, dtype=np.float64) * (-2.0 * math.log(500000.0) / head_dim))
    freq = freq.astype(np.float32).astype(np.float64)
    angle = (np.arange(context, dtype=np.float64)[:, None] * freq[None, :]).astype(np.float32)
    cosine, sine = np.cos(angle.astype(np.float64)), np.sin(angle.astype(np.float64))
    rest = np.concatenate([cosine, cosine, -sine, sine], axis=1).astype(np.float32)
    terms = []
    for _ in range(3):
        term = rest.astype(jnp.bfloat16)
        terms.append(term)
        rest = rest - term.astype(np.float32)
    return np.stack(terms)


def fused_device(
    tokens,
    query_weight,
    adapter_down_weight,
    adapter_up_weight,
    row_adapter_index,
    adapter_table_slot,
    lengths,
    cached_key_rows,
    cached_value_rows,
):
    rows, features = tokens.shape
    columns = query_weight.shape[1]
    n_ad = lax.axis_size("ad")
    n_tp = lax.axis_size("tp")
    held = adapter_down_weight.shape[0]
    rank = adapter_down_weight.shape[2]
    _, kv_heads, span, head_dim = cached_key_rows.shape
    cap = -(-(384 // n_ad) // 16) * 16

    depth = 1024
    slot_count = 4
    swapped = SWAPPED
    chunk = CHUNK
    heads = columns // head_dim
    spread_rows = rows - swapped
    chunks = spread_rows // chunk
    kv_mine = kv_heads // n_tp
    group = heads // kv_mine
    pairs = rows // 2
    spread_pairs = spread_rows // 2
    width = columns // kv_mine
    vmem = pl.BlockSpec(memory_space=pltpu.VMEM)
    smem = pl.BlockSpec(memory_space=pltpu.SMEM)
    anywhere = pl.BlockSpec(memory_space=pl.ANY)
    bf16, f32 = jnp.bfloat16, jnp.float32
    dma = pltpu.SemaphoreType.DMA
    groups = n_ad // 2
    rope = rope_table(n_tp * span, head_dim)
    results = pl.pallas_call(
        functools.partial(step_kernel, n_ad, n_tp, cap, rank, swapped, chunk),
        out_shape=(jax.ShapeDtypeStruct((rows, columns), bf16),) * 2,
        in_specs=[vmem] * 3 + [smem] + [anywhere] * 7,
        out_specs=(anywhere, anywhere),
        scratch_shapes=[
            pltpu.VMEM((rows, features), bf16),
            pltpu.VMEM(rope.shape, bf16),
            pltpu.VMEM((rows, LANES), bf16),
            pltpu.VMEM((rows, n_ad * cap), bf16),
            pltpu.VMEM((rows, head_dim), f32),
            pltpu.VMEM((rows, head_dim), f32),
            pltpu.VMEM((n_ad, cap, features + LANES), bf16),
            pltpu.VMEM((n_tp, rows, features), bf16),
            pltpu.VMEM((n_ad, cap, features + LANES), bf16),
            pltpu.VMEM((groups, 2 * cap, held * rank), bf16),
            pltpu.VMEM((kv_mine, n_ad, cap, width), bf16),
            pltpu.VMEM((kv_mine, n_ad, cap, width), bf16),
            pltpu.VMEM((groups, cap, LANES), f32),
            pltpu.VMEM((groups, n_tp, cap, LANES), f32),
            pltpu.VMEM((rows, columns), f32),
            pltpu.VMEM((slot_count, depth, columns), bf16),
            pltpu.VMEM((held * rank, features), bf16),
            pltpu.VMEM((held * rank, columns), bf16),
            pltpu.VMEM((rows, columns), bf16),
            pltpu.VMEM((rows, columns), bf16),
            pltpu.VMEM((kv_mine, rows, group, head_dim), f32),
            pltpu.VMEM((kv_mine, pairs, 2 * group, head_dim), bf16),
            pltpu.VMEM((kv_mine, swapped, n_tp, span, head_dim), bf16),
            pltpu.VMEM((kv_mine, swapped, n_tp, span, head_dim), bf16),
            pltpu.VMEM((kv_mine, n_tp, spread_pairs, 2 * group, head_dim), bf16),
            pltpu.VMEM((kv_mine, spread_rows, n_tp, span, head_dim), bf16),
            pltpu.VMEM((kv_mine, spread_rows, n_tp, span, head_dim), bf16),
            pltpu.VMEM((kv_mine, n_tp, spread_pairs, 2 * group, head_dim), bf16),
            pltpu.VMEM((kv_mine, chunks, 2, group, LANES), f32),
            pltpu.VMEM((kv_mine, n_tp, spread_pairs, 2 * group, head_dim), bf16),
            pltpu.VMEM((kv_mine, chunks, n_tp, 2, group, LANES), f32),
            dma((slot_count,)),
            dma((4,)),
            dma((kv_mine, 2, n_tp + 1)),
            dma((2 * kv_mine + kv_mine * chunks,)),
            dma((n_tp,)),
            dma((n_tp,)),
            dma((n_ad,)),
            dma((n_ad,)),
            dma((groups, n_tp)),
            dma((groups, n_tp)),
            dma((kv_mine, n_ad)),
            dma((kv_mine, n_ad)),
            dma((2, kv_mine, n_tp)),
            dma((2, kv_mine, n_tp)),
            dma((kv_mine, chunks, n_tp)),
            dma((kv_mine, chunks, n_tp)),
            dma((kv_mine, chunks, n_tp)),
            dma((kv_mine, chunks, n_tp)),
            dma((kv_mine, chunks, n_tp)),
            dma((kv_mine, chunks, n_tp)),
        ],
        compiler_params=pltpu.CompilerParams(
            collective_id=0, has_side_effects=True, vmem_limit_bytes=60 * 1024 * 1024
        ),
        name="step",
    )(
        row_adapter_index[None, :],
        adapter_table_slot[None, :],
        lengths[None, :],
        lengths,
        tokens,
        jnp.asarray(rope),
        query_weight,
        adapter_down_weight.transpose(0, 2, 1).reshape(held * rank, features),
        adapter_up_weight.reshape(held * rank, columns),
        cached_key_rows,
        cached_value_rows,
    )
    return pl.pallas_call(
        hand_over,
        out_shape=(jax.ShapeDtypeStruct((rows, columns), bf16),) * 2,
        in_specs=[anywhere] * 2,
        out_specs=(anywhere, anywhere),
        scratch_shapes=[pltpu.VMEM((2, rows, columns), bf16), dma((2, 2))],
        name="hand_over",
    )(*results)


def rotate(query, lengths):
    head_dim = query.shape[-1]
    half = head_dim // 2
    freq = jnp.exp(jnp.arange(half, dtype=jnp.float32) * (-2.0 * math.log(500000.0) / head_dim))
    angle = (lengths - 1).astype(jnp.float32)[:, None, None] * freq[None, None, :]
    cosine = jnp.cos(angle)
    sine = jnp.sin(angle)
    first = query[..., :half]
    second = query[..., half:]
    return jnp.concatenate(
        [first * cosine - second * sine, second * cosine + first * sine], axis=-1
    )


def lookup(ids, adapter_table_slot):
    table = jnp.arange(adapter_table_slot.shape[0], dtype=jnp.int32)
    return jnp.sum(
        jnp.where(ids[:, None] == table[None, :], adapter_table_slot[None, :], 0), axis=1
    )


def shrink_rows(input_rows, local_partial, adapter_down_weight):
    adapter_row_count = adapter_down_weight.shape[0]
    select_rows = (
        local_partial[:, None] == jnp.arange(adapter_row_count, dtype=jnp.int32)[None, :]
    ).astype(jnp.float32)
    update_terms = jnp.einsum(
        "nt,vtm->nvm", input_rows, adapter_down_weight, preferred_element_type=jnp.float32
    )
    return (select_rows, jnp.sum(update_terms * select_rows[:, :, None], axis=1))


def expand_rows(select_rows, reduced_rows, adapter_up_weight):
    spread_rows = (select_rows[:, :, None] * reduced_rows.astype(jnp.float32)[:, None, :]).astype(
        jnp.bfloat16
    )
    return jnp.einsum(
        "pow,owu->pu", spread_rows, adapter_up_weight, preferred_element_type=jnp.float32
    ).astype(jnp.bfloat16)


def per_device(
    tokens,
    query_weight,
    adapter_down_weight,
    adapter_up_weight,
    row_adapter_index,
    adapter_table_slot,
    lengths,
    cached_key_rows,
    cached_value_rows,
):
    rows = tokens.shape[0]
    columns = query_weight.shape[1]
    tp_count = lax.axis_size("tp")
    owner_partials = adapter_down_weight.shape[0]
    base = jnp.dot(
        lax.all_gather(tokens, "tp", axis=1, tiled=True),
        query_weight,
        preferred_element_type=jnp.float32,
    )
    combined_output, every_id = (
        lax.all_gather(tokens, "ad", axis=0, tiled=True),
        lax.all_gather(row_adapter_index, "ad", axis=0, tiled=True),
    )
    slots = lookup(every_id, adapter_table_slot)
    mine = slots // owner_partials == lax.axis_index("ad")
    local_partial = jnp.where(mine, slots % owner_partials, -1)
    select_rows, partial_value_sum = shrink_rows(
        combined_output, local_partial, adapter_down_weight
    )
    reduced_rows = lax.psum(partial_value_sum, "tp").astype(jnp.bfloat16)
    lowrank_change = expand_rows(select_rows, reduced_rows, adapter_up_weight)
    delta = lax.psum_scatter(
        lowrank_change.astype(jnp.float32).astype(jnp.bfloat16),
        "ad",
        scatter_dimension=0,
        tiled=True,
    ).astype(jnp.float32)
    head_dim = cached_key_rows.shape[3]
    query = (base + delta).reshape(rows, columns // head_dim, head_dim)
    queries = rotate(query, lengths).reshape(rows, columns).astype(jnp.bfloat16)
    every_head = lax.all_gather(queries, "tp", axis=1, tiled=True)
    kv_heads = cached_key_rows.shape[1]
    span = cached_key_rows.shape[2]
    grouped = every_head.reshape(rows, kv_heads, -1, head_dim)
    scores = jnp.einsum(
        "rkgd,rkpd->rkgp", grouped, cached_key_rows, preferred_element_type=jnp.float32
    ) * (1.0 / math.sqrt(head_dim))
    position = lax.axis_index("tp") * span + jnp.arange(span, dtype=jnp.int32)
    valid = (position[None, :] < lengths[:, None])[:, None, None, :]
    scores = jnp.where(valid, scores, -1e30)
    peak = jnp.max(scores, axis=-1)
    weights = jnp.where(valid, jnp.exp(scores - peak[..., None]), 0.0)
    total = jnp.sum(weights, axis=-1)
    partial_out = jnp.einsum(
        "rkgp,rkpd->rkgd",
        weights.astype(jnp.bfloat16),
        cached_value_rows,
        preferred_element_type=jnp.float32,
    ).astype(jnp.bfloat16)
    peaks, totals = (
        lax.all_to_all(
            peak.reshape(rows, tp_count, -1), "tp", split_axis=1, concat_axis=1, tiled=True
        ),
        lax.all_to_all(
            total.reshape(rows, tp_count, -1), "tp", split_axis=1, concat_axis=1, tiled=True
        ),
    )
    partials = lax.all_to_all(
        partial_out.reshape(rows, tp_count, -1), "tp", split_axis=1, concat_axis=1, tiled=True
    )
    highest = jnp.max(peaks, axis=1, keepdims=True)
    factor = jnp.exp(peaks - highest)
    numer = jnp.sum(
        factor[..., None] * partials.reshape(rows, tp_count, -1, head_dim).astype(jnp.float32),
        axis=1,
    )
    denom = jnp.sum(factor * totals, axis=1)
    attended = (numer / denom[..., None]).reshape(rows, columns).astype(jnp.bfloat16)
    return (queries, attended)


def solution(mesh):
    fits = mesh.shape["tp"] == 4 and mesh.shape["ad"] == 8
    return jax.shard_map(
        fused_device if fits else per_device,
        mesh=mesh,
        in_specs=(
            P("ad", "tp"),
            P(None, "tp"),
            P("ad", "tp", None),
            P("ad", None, "tp"),
            P("ad"),
            P(),
            P("ad"),
            P("ad", None, "tp", None),
            P("ad", None, "tp", None),
        ),
        out_specs=(P("ad", "tp"), P("ad", "tp")),
        check_vma=False,
    )
```

```python
import functools
import math

import jax
import jax.numpy as jnp
import numpy as np
from jax import lax
from jax.experimental import pallas as pl
from jax.experimental.pallas import tpu as pltpu
from jax.sharding import PartitionSpec as P

MESH = pl.DeviceIdType.MESH
LANES = 128
SWAPPED = 64
CHUNK = 32


def remote(src, dst, send_sem, recv_sem, axis, peer):
    return pltpu.make_async_remote_copy(
        src_ref=src,
        dst_ref=dst,
        send_sem=send_sem,
        recv_sem=recv_sem,
        device_id={axis: peer},
        device_id_type=MESH,
    )


def greet(counts):
    barrier = pltpu.get_barrier_semaphore()
    total = 0
    for axis, count in counts:
        me = lax.axis_index(axis)
        for d in range(1, count):
            pl.semaphore_signal(
                barrier, inc=1, device_id={axis: lax.rem(me + d, count)}, device_id_type=MESH
            )
            total += 1
    return total


def step_kernel(
    n_ad,
    n_tp,
    cap,
    rank,
    swapped,
    chunk,
    ids_ref,
    table_ref,
    lens_ref,
    lengths_ref,
    tokens_hbm,
    rope_hbm,
    weight_hbm,
    down_hbm,
    up_hbm,
    keys_hbm,
    values_hbm,
    out_hbm,
    att_hbm,
    tokens_ref,
    rope,
    mark,
    unpack,
    cosine,
    sine,
    packed,
    gathered,
    arrived,
    spread,
    outgoing,
    returned,
    part_send,
    part_recv,
    acc,
    weight_buf,
    down_buf,
    up_buf,
    out_ref,
    att_ref,
    heads_f32,
    heads_bf16,
    swap_keys,
    swap_values,
    every,
    keys,
    values,
    part,
    stat,
    part_in,
    stat_in,
    weight_sem,
    load_sem,
    cache_sem,
    done_sem,
    tok_send,
    tok_recv,
    row_send,
    row_recv,
    sum_send,
    sum_recv,
    ret_send,
    ret_recv,
    swap_send,
    swap_recv,
    q_send,
    q_recv,
    p_send,
    p_recv,
    s_send,
    s_recv,
):
    ad = lax.axis_index("ad")
    tp = lax.axis_index("tp")
    rows, features = tokens_ref.shape
    columns = out_ref.shape[1]
    depth = weight_buf.shape[1]
    slots = weight_buf.shape[0]
    subs = features // depth
    steps = n_tp * subs
    per = LANES // rank
    held_here = down_buf.shape[0] // rank
    pairs = down_buf.shape[0] // LANES
    tiles = down_buf.shape[0] // 256
    per_tile = 256 // LANES
    groups = n_ad // 2
    rows2 = 2 * cap
    kv_mine, _, pair_rows, size = heads_bf16.shape
    group = pair_rows // 2
    span = keys_hbm.shape[2]
    width = columns // kv_mine
    spread_rows = rows - swapped
    chunks = spread_rows // chunk
    units = chunk // 2
    context = n_tp * span
    scale = 1.0 / math.sqrt(size)
    f32, bf16 = jnp.float32, jnp.bfloat16

    def weight_copy(i):
        flip_x, flip_y = (i // subs) % 2, (i // subs) // 2
        column, line = lax.rem(tp, 2), tp // 2
        owner = 2 * (1 - line if flip_y else line) + (1 - column if flip_x else column)
        start = pl.multiple_of(owner * features + (i % subs) * depth, depth)
        return pltpu.make_async_copy(
            weight_hbm.at[pl.ds(start, depth), :], weight_buf.at[i % slots], weight_sem.at[i % slots]
        )

    tokens_copy = pltpu.make_async_copy(tokens_hbm, tokens_ref, load_sem.at[2])
    rope_copy = pltpu.make_async_copy(rope_hbm, rope, load_sem.at[3])
    down_copy = pltpu.make_async_copy(down_hbm, down_buf, load_sem.at[0])
    up_copy = pltpu.make_async_copy(up_hbm, up_buf, load_sem.at[1])
    tokens_copy.start()
    down_copy.start()
    for i in range(slots):
        weight_copy(i).start()
    rope_copy.start()
    up_copy.start()
    early = pl.ds(0, swapped)
    late = pl.ds(swapped, spread_rows)
    cache_copies = []
    for j in range(kv_mine):
        for which, source, near, far in (
            (0, keys_hbm, swap_keys, keys),
            (1, values_hbm, swap_values, values),
        ):
            cache_copies.append(
                pltpu.make_async_copy(
                    source.at[early, tp * kv_mine + j], near.at[j, :, 0], cache_sem.at[j, which, n_tp]
                )
            )
            for t in range(n_tp):
                cache_copies.append(
                    pltpu.make_async_copy(
                        source.at[late, t * kv_mine + j], far.at[j, :, t], cache_sem.at[j, which, t]
                    )
                )

    greetings = greet((("ad", n_ad), ("tp", n_tp)))

    index0 = lax.broadcasted_iota(jnp.int32, (rows, rows), 0)
    index1 = lax.broadcasted_iota(jnp.int32, (rows, rows), 1)
    diagonal = index0 == index1

    def to_column(row):
        return jnp.sum(jnp.where(diagonal, row, 0.0), axis=1, keepdims=True)

    def to_row(column):
        return jnp.sum(jnp.where(diagonal, column, 0.0), axis=0, keepdims=True)

    adapters = table_ref.shape[1]
    ids_column = to_column(ids_ref[...].astype(f32))
    adapter = lax.broadcasted_iota(jnp.int32, (rows, adapters), 1).astype(f32)
    slot_column = jnp.sum(
        jnp.where(ids_column == adapter, table_ref[...].astype(f32), 0.0), axis=1, keepdims=True
    )
    owner_column = jnp.floor((slot_column + 0.5) * (1.0 / held_here))
    owner_row = to_row(owner_column)
    same = owner_column == owner_row
    place_column = owner_column * cap + jnp.sum(
        jnp.where(same & (index1 < index0), 1.0, 0.0), axis=1, keepdims=True
    )
    place_row = owner_row * cap + jnp.sum(
        jnp.where(same & (index0 < index1), 1.0, 0.0), axis=0, keepdims=True
    )
    mark[...] = jnp.broadcast_to(slot_column - owner_column * held_here + 1.0, (rows, LANES)).astype(
        bf16
    )
    cell_row = lax.broadcasted_iota(jnp.int32, (cap, rows), 0)

    def pack_into(d, peer, target):
        pick = ((cell_row + peer * cap).astype(f32) == place_row).astype(bf16)

        @pl.loop(0, features // 512)
        def _(c):
            at = pl.ds(pl.multiple_of(c * 512, 512), 512)
            target[d, :, at] = jnp.dot(
                pick, tokens_ref[:, at], preferred_element_type=f32
            ).astype(bf16)

        target[d, :, pl.ds(features, LANES)] = jnp.dot(
            pick, mark[...], preferred_element_type=f32
        ).astype(bf16)

    column, line = lax.rem(tp, 2), tp // 2
    beside = [tp, 2 * line + 1 - column, 2 * (1 - line) + column, 2 * (1 - line) + 1 - column]
    halves = [pl.ds(0, rows // 2), pl.ds(rows // 2, rows // 2)]
    tok_copies = {}

    def send_tokens(e, source, h, via):
        copy = remote(
            source.at[halves[h]],
            gathered.at[e, halves[h]],
            tok_send.at[e, h],
            tok_recv.at[e, h],
            "tp",
            beside[via],
        )
        copy.start()
        tok_copies[e, h] = copy

    def forward_tokens():
        tok_copies[2, 0].wait_recv()
        send_tokens(3, gathered.at[2], 0, 1)
        tok_copies[1, 1].wait_recv()
        send_tokens(3, gathered.at[1], 1, 2)

    tokens_copy.wait()
    order = sorted(range(1, n_ad), key=lambda d: abs(d - n_ad // 2))
    row_copies = {}
    for d in order:
        peer = lax.rem(ad + d, n_ad)
        pack_into(d, peer, packed)
        if d == order[0]:
            pl.semaphore_wait(pltpu.get_barrier_semaphore(), greetings)
        copy = remote(packed.at[d], arrived.at[d], row_send.at[d], row_recv.at[d], "ad", peer)
        copy.start()
        row_copies[d] = copy
        if d == order[0]:
            for h in range(2):
                send_tokens(2, tokens_ref, h, 2)
                send_tokens(1, tokens_ref, 1 - h, 1)
    pack_into(0, ad, arrived)

    cells = lax.broadcasted_iota(jnp.int32, (rows, n_ad * cap), 1).astype(f32)
    unpack[...] = (cells == place_column).astype(bf16)
    moment = to_column(lens_ref[...].astype(f32)) - 1.0
    chosen = (lax.broadcasted_iota(jnp.int32, (rows, context), 1).astype(f32) == moment).astype(bf16)
    rope_copy.wait()
    turn = jnp.dot(chosen, rope[0], preferred_element_type=f32)
    for k in range(1, rope.shape[0]):
        turn = turn + jnp.dot(chosen, rope[k], preferred_element_type=f32)
    cosine[...] = turn[:, :size]
    sine[...] = turn[:, size:]

    swap_copies = []

    def swap(which, source, target):
        for j in range(kv_mine):
            for e in range(1, n_tp):
                peer = lax.rem(tp + e, n_tp)
                copy = remote(
                    source.at[early, peer * kv_mine + j],
                    target.at[j, :, e],
                    swap_send.at[which, j, e],
                    swap_recv.at[which, j, e],
                    "tp",
                    peer,
                )
                copy.start()
                swap_copies.append((j, copy))

    def base_chunk(e):
        if e == 1:
            tok_copies[1, 0].wait_recv()
        if e == 2:
            tok_copies[2, 1].wait_recv()
        if e == 3:
            tok_copies[3, 0].wait_recv()
            tok_copies[3, 1].wait_recv()
        block = tokens_ref if e == 0 else gathered.at[e]
        for sub in range(subs):
            i = e * subs + sub
            weight_copy(i).wait()

            @pl.loop(0, columns // 256)
            def _(c):
                at = pl.ds(pl.multiple_of(c * 256, 256), 256)
                product = jnp.dot(
                    block[:, pl.ds(sub * depth, depth)],
                    weight_buf[i % slots, :, at],
                    preferred_element_type=f32,
                )
                if i == 0:
                    acc[:, at] = product
                else:
                    acc[:, at] += product

            if i + slots < steps:
                weight_copy(i + slots).start()

    lane2 = lax.broadcasted_iota(jnp.int32, (rows2, LANES), 1)
    part_of = (lane2 // rank).astype(f32)
    lane1 = lax.broadcasted_iota(jnp.int32, (cap, LANES), 1)
    sum_copies = {}
    ret_copies = {}

    def ids_of(g):
        return (
            arrived[pl.ds(2 * g, 2), :, pl.ds(features, LANES)].reshape(rows2, LANES).astype(f32)
            - 1.0
        )

    def shrink(g):
        for d in (2 * g, 2 * g + 1):
            if d:
                row_copies[d].wait_recv()
        if g == 0:
            down_copy.wait()
        ids = ids_of(g) - part_of

        def tile(t, total):
            product = lax.dot_general(
                arrived[pl.ds(2 * g, 2), :, pl.ds(0, features)].reshape(rows2, features),
                down_buf[pl.ds(pl.multiple_of(t * 256, 256), 256), :],
                (((1,), (1,)), ((), ())),
                preferred_element_type=f32,
            )
            for k in range(per_tile):
                want = ((t * per_tile + k) * per).astype(f32)
                total = total + jnp.where(
                    ids == want, product[:, k * LANES : (k + 1) * LANES], 0.0
                )
            return total

        total = lax.fori_loop(0, tiles, tile, jnp.zeros((rows2, LANES), f32))
        total = total + pltpu.roll(total, rank, 1)
        part_send[g] = jnp.where(lane1 < rank, total[:cap], total[cap:])
        for e in range(1, n_tp):
            copy = remote(
                part_send.at[g],
                part_recv.at[g, e],
                sum_send.at[g, e],
                sum_recv.at[g, e],
                "tp",
                lax.rem(tp + e, n_tp),
            )
            copy.start()
            sum_copies[g, e] = copy

    def expand(g, j):
        if j == 0:
            if g == 0:
                up_copy.wait()
            total = part_send[g]
            for e in range(1, n_tp):
                sum_copies[g, e].wait_recv()
                total = total + part_recv[g, e]
            turned = pltpu.roll(total, rank, 1)
            both = jnp.concatenate(
                [jnp.where(lane1 < rank, total, turned), jnp.where(lane1 < rank, turned, total)],
                axis=0,
            )
            ids = ids_of(g) - part_of
            for k in range(pairs):
                spread[g, :, k * LANES : (k + 1) * LANES] = jnp.where(
                    ids == float(k * per), both, 0.0
                ).astype(bf16)

        @pl.loop(0, width // 256)
        def _(c):
            at = pl.ds(pl.multiple_of(c * 256, 256), 256)
            source = pl.ds(pl.multiple_of(j * width + c * 256, 256), 256)
            change = jnp.dot(spread[g], up_buf[:, source], preferred_element_type=f32)
            outgoing[j, pl.ds(2 * g, 2), :, at] = change.astype(bf16).reshape(2, cap, 256)

        for d in (2 * g, 2 * g + 1):
            if d:
                copy = remote(
                    outgoing.at[j, d],
                    returned.at[j, ad],
                    ret_send.at[j, d],
                    ret_recv.at[j, d],
                    "ad",
                    lax.rem(ad + n_ad - d, n_ad),
                )
                if j == 0:
                    copy.start()
                ret_copies[j, d] = copy
            else:
                returned[j, ad] = outgoing[j, 0]

    done_copies = []

    def finish(k, where, source, target):
        copy = pltpu.make_async_copy(source.at[where], target.at[where], done_sem.at[k])
        copy.start()
        done_copies.append(copy)

    sends = {}
    late_pairs = pl.ds(swapped // 2, spread_rows // 2)

    def rotate(j):
        for d in range(1, n_ad):
            ret_copies[j, d].wait_recv()
        for c in range(width // 256):
            at = pl.ds(j * width + c * 256, 256)
            delta = jnp.dot(
                unpack[...],
                returned[j, :, :, pl.ds(c * 256, 256)].reshape(n_ad * cap, 256),
                preferred_element_type=f32,
            )
            query = acc[:, at] + delta
            pieces = []
            for h in range(256 // size):
                one = query[:, h * size : (h + 1) * size]
                piece = one * cosine[...] + pltpu.roll(one, size // 2, 1) * sine[...]
                heads_f32[j, :, c * (256 // size) + h, :] = piece
                pieces.append(piece)
            out_ref[:, at] = jnp.concatenate(pieces, axis=1).astype(bf16)
        heads_bf16[j] = heads_f32[j].reshape(rows // 2, pair_rows, size).astype(bf16)
        for c in range(chunks):
            for e in range(1, n_tp):
                copy = remote(
                    heads_bf16.at[j, pl.ds(swapped // 2 + c * units, units)],
                    every.at[j, tp, pl.ds(c * units, units)],
                    q_send.at[j, c, e],
                    q_recv.at[j, c, e],
                    "tp",
                    lax.rem(tp + e, n_tp),
                )
                copy.start()
                sends[j, c, e] = copy
        every[j, tp] = heads_bf16[j, late_pairs]
        finish(j, (slice(None), pl.ds(j * width, width)), out_ref, out_hbm)

    lane = lax.broadcasted_iota(jnp.int32, (group, LANES), 1)
    half = LANES // 2

    def top_of(x, extent):
        k = extent // 2
        while k:
            flat = x.reshape(-1, LANES)
            up = pltpu.roll(flat, k, 1).reshape(x.shape)
            down = pltpu.roll(flat, LANES - k, 1).reshape(x.shape)
            x = jnp.maximum(x, jnp.where((lane // k) % 2 == 1, up, down))
            k //= 2
        return x

    def settle(j, first, count, k):
        at = pl.ds(first, count)
        for h in range(group):
            att_ref[at, j * width + h * size : j * width + (h + 1) * size] = heads_f32[
                j, at, h, :
            ].astype(bf16)
        finish(k, (at, pl.ds(j * width, width)), att_ref, att_hbm)

    near_place = lax.rem(tp + n_tp - (lane % half) // span, n_tp) * span + lane % span
    far_place = tp * span + lane % span
    seat = lane % span
    seat_of = lane // span
    ones = jnp.ones((LANES, LANES), bf16)
    belongs = (
        lax.broadcasted_iota(jnp.int32, (LANES, LANES), 0) // span
        == lax.broadcasted_iota(jnp.int32, (LANES, LANES), 1) // span
    ).astype(bf16)

    def attend_near(j):
        for k, copy in swap_copies:
            if k == j:
                copy.wait_recv()

        batch = 8

        @pl.loop(0, swapped // (2 * batch))
        def _(b):
            merged, limits = [], []
            for u in range(batch):
                p = b * batch + u
                score = lax.dot_general(
                    heads_bf16[j, p],
                    swap_keys[j, pl.ds(2 * p, 2)].reshape(LANES, size),
                    (((1,), (1,)), ((), ())),
                    preferred_element_type=f32,
                )
                merged.append(jnp.where(lane < half, score[:group], score[group:]))
                limits.append(
                    jnp.where(lane < half, lengths_ref[2 * p], lengths_ref[2 * p + 1])
                )
            valid = near_place[None] < jnp.stack(limits)
            score = jnp.where(valid, jnp.stack(merged) * scale, -1e30)
            peak = top_of(score, half)
            weight = jnp.where(valid, jnp.exp(score - peak), 0.0)
            first = jnp.where(lane < half, weight, 0.0)
            both = jnp.concatenate([first, weight - first], axis=1).astype(bf16)
            total = jnp.dot(
                both.reshape(batch * pair_rows, LANES), ones, preferred_element_type=f32
            )
            for u in range(batch):
                p = b * batch + u
                result = jnp.dot(
                    both[u],
                    swap_values[j, pl.ds(2 * p, 2)].reshape(LANES, size),
                    preferred_element_type=f32,
                )
                result = result / total[u * pair_rows : (u + 1) * pair_rows]
                heads_f32[j, pl.ds(2 * p, 2)] = result.reshape(2, group, size)

        settle(j, 0, swapped, kv_mine + j)

    unroll = 8
    outs = []

    def attend(j, c):
        for e in range(1, n_tp):
            sends[j, c, e].wait_recv()

        def some(b, held):
            peaks, totals = held
            merged, limits = [], []
            for u in range(unroll):
                p = c * units + b * unroll + u
                score = lax.dot_general(
                    jnp.concatenate([every[j, t, p] for t in range(n_tp)], axis=0),
                    keys[j, pl.ds(2 * p, 2)].reshape(LANES, size),
                    (((1,), (1,)), ((), ())),
                    preferred_element_type=f32,
                )
                one = score[:group]
                for i in range(2):
                    for t in range(n_tp):
                        at = t * pair_rows + i * group
                        one = jnp.where(seat_of == i * n_tp + t, score[at : at + group], one)
                merged.append(one)
                limits.append(
                    jnp.where(
                        lane < half, lengths_ref[swapped + 2 * p], lengths_ref[swapped + 2 * p + 1]
                    )
                )
            valid = far_place[None] < jnp.stack(limits)
            score = jnp.where(valid, jnp.stack(merged) * scale, -1e30)
            peak = top_of(score, span)
            weight = jnp.where(valid, jnp.exp(score - peak), 0.0)
            total = jnp.dot(
                weight.reshape(unroll * group, LANES).astype(bf16),
                belongs,
                preferred_element_type=f32,
            )
            for u in range(unroll):
                local = b * unroll + u
                p = c * units + local
                blocks = [
                    jnp.where(seat_of == i * n_tp + t, weight[u], 0.0)
                    for t in range(n_tp)
                    for i in range(2)
                ]
                result = jnp.dot(
                    jnp.concatenate(blocks, axis=0).astype(bf16),
                    values[j, pl.ds(2 * p, 2)].reshape(LANES, size),
                    preferred_element_type=f32,
                ).astype(bf16)
                for t in range(n_tp):
                    part[j, t, p] = result[t * pair_rows : (t + 1) * pair_rows]
                peaks = jnp.where(seat == local, peak[u], peaks)
                totals = jnp.where(seat == local, total[u * group : (u + 1) * group], totals)
            return peaks, totals

        zero = jnp.zeros((group, LANES), f32)
        peaks, totals = lax.fori_loop(0, units // unroll, some, (zero, zero))
        stat[j, c, 0] = peaks
        stat[j, c, 1] = totals
        at = pl.ds(c * units, units)
        for e in range(1, n_tp):
            peer = lax.rem(tp + e, n_tp)
            s = remote(
                stat.at[j, c], stat_in.at[j, c, e], s_send.at[j, c, e], s_recv.at[j, c, e], "tp", peer
            )
            p = remote(
                part.at[j, peer, at],
                part_in.at[j, e, at],
                p_send.at[j, c, e],
                p_recv.at[j, c, e],
                "tp",
                peer,
            )
            s.start()
            p.start()
            outs.append((j, c, s))
            outs.append((j, c, p))
        part_in[j, 0, at] = part[j, tp, at]
        stat_in[j, c, 0] = stat[j, c]

    def combine(j, c):
        for k, b, copy in outs:
            if (k, b) == (j, c):
                copy.wait_recv()
        peaks = [stat_in[j, c, e, 0] for e in range(n_tp)]
        top = functools.reduce(jnp.maximum, peaks)
        factors = [jnp.exp(s - top) for s in peaks]
        denom = sum(f * stat_in[j, c, e, 1] for e, f in enumerate(factors))
        shares = [f / denom for f in factors]

        @pl.loop(0, units // unroll)
        def _(b):
            for u in range(unroll):
                local = b * unroll + u
                p = c * units + local
                mine = tp * span + local
                result = jnp.zeros((pair_rows, size), f32)
                for e in range(n_tp):
                    share = jnp.concatenate(
                        [
                            jnp.sum(
                                jnp.where(lane == i * half + mine, shares[e], 0.0),
                                axis=1,
                                keepdims=True,
                            )
                            for i in range(2)
                        ],
                        axis=0,
                    )
                    result = result + share * part_in[j, e, p].astype(f32)
                heads_f32[j, pl.ds(swapped + 2 * p, 2)] = result.reshape(2, group, size)

        settle(j, swapped + c * chunk, chunk, 2 * kv_mine + j * chunks + c)

    base_chunk(0)
    forward_tokens()
    swap(0, keys_hbm, swap_keys)
    base_chunk(1)
    base_chunk(2)
    for copy in cache_copies:
        copy.start()
    for g in range(groups):
        shrink(g)
    swap(1, values_hbm, swap_values)
    base_chunk(3)
    for j in range(kv_mine):
        for g in range(groups):
            expand(g, j)
    for j in range(1, kv_mine):
        for d in sorted(range(1, n_ad), key=lambda d: abs(d - n_ad // 2), reverse=True):
            ret_copies[j - 1, d].wait_send()
            ret_copies[j, d].start()
    for copy in cache_copies:
        copy.wait()
    rotate(0)
    attend_near(0)
    for c in range(chunks):
        attend(0, c)
    for c in range(chunks - 1):
        combine(0, c)
    rotate(1)
    attend_near(1)
    for c in range(chunks):
        attend(1, c)
    combine(0, chunks - 1)
    for c in range(chunks):
        combine(1, c)

    for copy in list(row_copies.values()) + list(tok_copies.values()) + list(sum_copies.values()):
        copy.wait_send()
    for d in range(1, n_ad):
        ret_copies[kv_mine - 1, d].wait_send()
    for _, copy in swap_copies:
        copy.wait_send()
    for copy in list(sends.values()) + [copy for _, _, copy in outs]:
        copy.wait_send()
    for copy in done_copies:
        copy.wait()


def hand_over(first_hbm, second_hbm, out_hbm, att_hbm, held, sem):
    loads = []
    for k, source in enumerate((first_hbm, second_hbm)):
        copy = pltpu.make_async_copy(source, held.at[k], sem.at[0, k])
        copy.start()
        loads.append(copy)
    stores = []
    for k, target in enumerate((out_hbm, att_hbm)):
        loads[k].wait()
        copy = pltpu.make_async_copy(held.at[k], target, sem.at[1, k])
        copy.start()
        stores.append(copy)
    for copy in stores:
        copy.wait()


def rope_table(context, head_dim):
    half = head_dim // 2
    freq = np.exp(np.arange(half, dtype=np.float64) * (-2.0 * math.log(500000.0) / head_dim))
    freq = freq.astype(np.float32).astype(np.float64)
    angle = (np.arange(context, dtype=np.float64)[:, None] * freq[None, :]).astype(np.float32)
    cosine, sine = np.cos(angle.astype(np.float64)), np.sin(angle.astype(np.float64))
    rest = np.concatenate([cosine, cosine, -sine, sine], axis=1).astype(np.float32)
    terms = []
    for _ in range(3):
        term = rest.astype(jnp.bfloat16)
        terms.append(term)
        rest = rest - term.astype(np.float32)
    return np.stack(terms)


def fused_device(
    tokens,
    query_weight,
    adapter_down_weight,
    adapter_up_weight,
    row_adapter_index,
    adapter_table_slot,
    lengths,
    cached_key_rows,
    cached_value_rows,
):
    rows, features = tokens.shape
    columns = query_weight.shape[1]
    n_ad = lax.axis_size("ad")
    n_tp = lax.axis_size("tp")
    held = adapter_down_weight.shape[0]
    rank = adapter_down_weight.shape[2]
    _, kv_heads, span, head_dim = cached_key_rows.shape
    cap = -(-(384 // n_ad) // 16) * 16

    depth = 1024
    slot_count = 4
    swapped = SWAPPED
    chunk = CHUNK
    heads = columns // head_dim
    spread_rows = rows - swapped
    chunks = spread_rows // chunk
    kv_mine = kv_heads // n_tp
    group = heads // kv_mine
    pairs = rows // 2
    spread_pairs = spread_rows // 2
    width = columns // kv_mine
    vmem = pl.BlockSpec(memory_space=pltpu.VMEM)
    smem = pl.BlockSpec(memory_space=pltpu.SMEM)
    anywhere = pl.BlockSpec(memory_space=pl.ANY)
    bf16, f32 = jnp.bfloat16, jnp.float32
    dma = pltpu.SemaphoreType.DMA
    groups = n_ad // 2
    rope = rope_table(n_tp * span, head_dim)
    results = pl.pallas_call(
        functools.partial(step_kernel, n_ad, n_tp, cap, rank, swapped, chunk),
        out_shape=(jax.ShapeDtypeStruct((rows, columns), bf16),) * 2,
        in_specs=[vmem] * 3 + [smem] + [anywhere] * 7,
        out_specs=(anywhere, anywhere),
        scratch_shapes=[
            pltpu.VMEM((rows, features), bf16),
            pltpu.VMEM(rope.shape, bf16),
            pltpu.VMEM((rows, LANES), bf16),
            pltpu.VMEM((rows, n_ad * cap), bf16),
            pltpu.VMEM((rows, head_dim), f32),
            pltpu.VMEM((rows, head_dim), f32),
            pltpu.VMEM((n_ad, cap, features + LANES), bf16),
            pltpu.VMEM((n_tp, rows, features), bf16),
            pltpu.VMEM((n_ad, cap, features + LANES), bf16),
            pltpu.VMEM((groups, 2 * cap, held * rank), bf16),
            pltpu.VMEM((kv_mine, n_ad, cap, width), bf16),
            pltpu.VMEM((kv_mine, n_ad, cap, width), bf16),
            pltpu.VMEM((groups, cap, LANES), f32),
            pltpu.VMEM((groups, n_tp, cap, LANES), f32),
            pltpu.VMEM((rows, columns), f32),
            pltpu.VMEM((slot_count, depth, columns), bf16),
            pltpu.VMEM((held * rank, features), bf16),
            pltpu.VMEM((held * rank, columns), bf16),
            pltpu.VMEM((rows, columns), bf16),
            pltpu.VMEM((rows, columns), bf16),
            pltpu.VMEM((kv_mine, rows, group, head_dim), f32),
            pltpu.VMEM((kv_mine, pairs, 2 * group, head_dim), bf16),
            pltpu.VMEM((kv_mine, swapped, n_tp, span, head_dim), bf16),
            pltpu.VMEM((kv_mine, swapped, n_tp, span, head_dim), bf16),
            pltpu.VMEM((kv_mine, n_tp, spread_pairs, 2 * group, head_dim), bf16),
            pltpu.VMEM((kv_mine, spread_rows, n_tp, span, head_dim), bf16),
            pltpu.VMEM((kv_mine, spread_rows, n_tp, span, head_dim), bf16),
            pltpu.VMEM((kv_mine, n_tp, spread_pairs, 2 * group, head_dim), bf16),
            pltpu.VMEM((kv_mine, chunks, 2, group, LANES), f32),
            pltpu.VMEM((kv_mine, n_tp, spread_pairs, 2 * group, head_dim), bf16),
            pltpu.VMEM((kv_mine, chunks, n_tp, 2, group, LANES), f32),
            dma((slot_count,)),
            dma((4,)),
            dma((kv_mine, 2, n_tp + 1)),
            dma((2 * kv_mine + kv_mine * chunks,)),
            dma((n_tp, 2)),
            dma((n_tp, 2)),
            dma((n_ad,)),
            dma((n_ad,)),
            dma((groups, n_tp)),
            dma((groups, n_tp)),
            dma((kv_mine, n_ad)),
            dma((kv_mine, n_ad)),
            dma((2, kv_mine, n_tp)),
            dma((2, kv_mine, n_tp)),
            dma((kv_mine, chunks, n_tp)),
            dma((kv_mine, chunks, n_tp)),
            dma((kv_mine, chunks, n_tp)),
            dma((kv_mine, chunks, n_tp)),
            dma((kv_mine, chunks, n_tp)),
            dma((kv_mine, chunks, n_tp)),
        ],
        compiler_params=pltpu.CompilerParams(
            collective_id=0, has_side_effects=True, vmem_limit_bytes=60 * 1024 * 1024
        ),
        name="step",
    )(
        row_adapter_index[None, :],
        adapter_table_slot[None, :],
        lengths[None, :],
        lengths,
        tokens,
        jnp.asarray(rope),
        query_weight,
        adapter_down_weight.transpose(0, 2, 1).reshape(held * rank, features),
        adapter_up_weight.reshape(held * rank, columns),
        cached_key_rows,
        cached_value_rows,
    )
    return pl.pallas_call(
        hand_over,
        out_shape=(jax.ShapeDtypeStruct((rows, columns), bf16),) * 2,
        in_specs=[anywhere] * 2,
        out_specs=(anywhere, anywhere),
        scratch_shapes=[pltpu.VMEM((2, rows, columns), bf16), dma((2, 2))],
        name="hand_over",
    )(*results)


def rotate(query, lengths):
    head_dim = query.shape[-1]
    half = head_dim // 2
    freq = jnp.exp(jnp.arange(half, dtype=jnp.float32) * (-2.0 * math.log(500000.0) / head_dim))
    angle = (lengths - 1).astype(jnp.float32)[:, None, None] * freq[None, None, :]
    cosine = jnp.cos(angle)
    sine = jnp.sin(angle)
    first = query[..., :half]
    second = query[..., half:]
    return jnp.concatenate(
        [first * cosine - second * sine, second * cosine + first * sine], axis=-1
    )


def lookup(ids, adapter_table_slot):
    table = jnp.arange(adapter_table_slot.shape[0], dtype=jnp.int32)
    return jnp.sum(
        jnp.where(ids[:, None] == table[None, :], adapter_table_slot[None, :], 0), axis=1
    )


def shrink_rows(input_rows, local_partial, adapter_down_weight):
    adapter_row_count = adapter_down_weight.shape[0]
    select_rows = (
        local_partial[:, None] == jnp.arange(adapter_row_count, dtype=jnp.int32)[None, :]
    ).astype(jnp.float32)
    update_terms = jnp.einsum(
        "nt,vtm->nvm", input_rows, adapter_down_weight, preferred_element_type=jnp.float32
    )
    return (select_rows, jnp.sum(update_terms * select_rows[:, :, None], axis=1))


def expand_rows(select_rows, reduced_rows, adapter_up_weight):
    spread_rows = (select_rows[:, :, None] * reduced_rows.astype(jnp.float32)[:, None, :]).astype(
        jnp.bfloat16
    )
    return jnp.einsum(
        "pow,owu->pu", spread_rows, adapter_up_weight, preferred_element_type=jnp.float32
    ).astype(jnp.bfloat16)


def per_device(
    tokens,
    query_weight,
    adapter_down_weight,
    adapter_up_weight,
    row_adapter_index,
    adapter_table_slot,
    lengths,
    cached_key_rows,
    cached_value_rows,
):
    rows = tokens.shape[0]
    columns = query_weight.shape[1]
    tp_count = lax.axis_size("tp")
    owner_partials = adapter_down_weight.shape[0]
    base = jnp.dot(
        lax.all_gather(tokens, "tp", axis=1, tiled=True),
        query_weight,
        preferred_element_type=jnp.float32,
    )
    combined_output, every_id = (
        lax.all_gather(tokens, "ad", axis=0, tiled=True),
        lax.all_gather(row_adapter_index, "ad", axis=0, tiled=True),
    )
    slots = lookup(every_id, adapter_table_slot)
    mine = slots // owner_partials == lax.axis_index("ad")
    local_partial = jnp.where(mine, slots % owner_partials, -1)
    select_rows, partial_value_sum = shrink_rows(
        combined_output, local_partial, adapter_down_weight
    )
    reduced_rows = lax.psum(partial_value_sum, "tp").astype(jnp.bfloat16)
    lowrank_change = expand_rows(select_rows, reduced_rows, adapter_up_weight)
    delta = lax.psum_scatter(
        lowrank_change.astype(jnp.float32).astype(jnp.bfloat16),
        "ad",
        scatter_dimension=0,
        tiled=True,
    ).astype(jnp.float32)
    head_dim = cached_key_rows.shape[3]
    query = (base + delta).reshape(rows, columns // head_dim, head_dim)
    queries = rotate(query, lengths).reshape(rows, columns).astype(jnp.bfloat16)
    every_head = lax.all_gather(queries, "tp", axis=1, tiled=True)
    kv_heads = cached_key_rows.shape[1]
    span = cached_key_rows.shape[2]
    grouped = every_head.reshape(rows, kv_heads, -1, head_dim)
    scores = jnp.einsum(
        "rkgd,rkpd->rkgp", grouped, cached_key_rows, preferred_element_type=jnp.float32
    ) * (1.0 / math.sqrt(head_dim))
    position = lax.axis_index("tp") * span + jnp.arange(span, dtype=jnp.int32)
    valid = (position[None, :] < lengths[:, None])[:, None, None, :]
    scores = jnp.where(valid, scores, -1e30)
    peak = jnp.max(scores, axis=-1)
    weights = jnp.where(valid, jnp.exp(scores - peak[..., None]), 0.0)
    total = jnp.sum(weights, axis=-1)
    partial_out = jnp.einsum(
        "rkgp,rkpd->rkgd",
        weights.astype(jnp.bfloat16),
        cached_value_rows,
        preferred_element_type=jnp.float32,
    ).astype(jnp.bfloat16)
    peaks, totals = (
        lax.all_to_all(
            peak.reshape(rows, tp_count, -1), "tp", split_axis=1, concat_axis=1, tiled=True
        ),
        lax.all_to_all(
            total.reshape(rows, tp_count, -1), "tp", split_axis=1, concat_axis=1, tiled=True
        ),
    )
    partials = lax.all_to_all(
        partial_out.reshape(rows, tp_count, -1), "tp", split_axis=1, concat_axis=1, tiled=True
    )
    highest = jnp.max(peaks, axis=1, keepdims=True)
    factor = jnp.exp(peaks - highest)
    numer = jnp.sum(
        factor[..., None] * partials.reshape(rows, tp_count, -1, head_dim).astype(jnp.float32),
        axis=1,
    )
    denom = jnp.sum(factor * totals, axis=1)
    attended = (numer / denom[..., None]).reshape(rows, columns).astype(jnp.bfloat16)
    return (queries, attended)


def solution(mesh):
    fits = mesh.shape["tp"] == 4 and mesh.shape["ad"] == 8
    return jax.shard_map(
        fused_device if fits else per_device,
        mesh=mesh,
        in_specs=(
            P("ad", "tp"),
            P(None, "tp"),
            P("ad", "tp", None),
            P("ad", None, "tp"),
            P("ad"),
            P(),
            P("ad"),
            P("ad", None, "tp", None),
            P("ad", None, "tp", None),
        ),
        out_specs=(P("ad", "tp"), P("ad", "tp")),
        check_vma=False,
    )
```

```python
import functools
import math

import jax
import jax.numpy as jnp
import numpy as np
from jax import lax
from jax.experimental import pallas as pl
from jax.experimental.pallas import tpu as pltpu
from jax.sharding import PartitionSpec as P

MESH = pl.DeviceIdType.MESH
LANES = 128
SWAPPED = 64
CHUNK = 32


def remote(src, dst, send_sem, recv_sem, axis, peer):
    return pltpu.make_async_remote_copy(
        src_ref=src,
        dst_ref=dst,
        send_sem=send_sem,
        recv_sem=recv_sem,
        device_id={axis: peer},
        device_id_type=MESH,
    )


def greet(counts):
    barrier = pltpu.get_barrier_semaphore()
    total = 0
    for axis, count in counts:
        me = lax.axis_index(axis)
        for d in range(1, count):
            pl.semaphore_signal(
                barrier, inc=1, device_id={axis: lax.rem(me + d, count)}, device_id_type=MESH
            )
            total += 1
    return total


def step_kernel(
    n_ad,
    n_tp,
    cap,
    rank,
    swapped,
    chunk,
    ids_ref,
    table_ref,
    lens_ref,
    lengths_ref,
    tokens_hbm,
    rope_hbm,
    weight_hbm,
    down_hbm,
    up_hbm,
    keys_hbm,
    values_hbm,
    out_hbm,
    att_hbm,
    tokens_ref,
    rope,
    mark,
    unpack,
    cosine,
    sine,
    packed,
    gathered,
    arrived,
    spread,
    outgoing,
    returned,
    part_send,
    part_recv,
    acc,
    weight_buf,
    down_buf,
    up_buf,
    out_ref,
    att_ref,
    heads_f32,
    heads_bf16,
    swap_keys,
    swap_values,
    every,
    keys,
    values,
    part,
    stat,
    part_in,
    stat_in,
    weight_sem,
    load_sem,
    cache_sem,
    done_sem,
    tok_send,
    tok_recv,
    row_send,
    row_recv,
    sum_send,
    sum_recv,
    ret_send,
    ret_recv,
    swap_send,
    swap_recv,
    q_send,
    q_recv,
    p_send,
    p_recv,
    s_send,
    s_recv,
):
    ad = lax.axis_index("ad")
    tp = lax.axis_index("tp")
    rows, features = tokens_ref.shape
    columns = out_ref.shape[1]
    depth = weight_buf.shape[1]
    slots = weight_buf.shape[0]
    subs = features // depth
    steps = n_tp * subs
    per = LANES // rank
    held_here = down_buf.shape[0] // rank
    pairs = down_buf.shape[0] // LANES
    tiles = down_buf.shape[0] // 256
    per_tile = 256 // LANES
    groups = n_ad // 2
    rows2 = 2 * cap
    kv_mine, _, pair_rows, size = heads_bf16.shape
    group = pair_rows // 2
    span = keys_hbm.shape[2]
    width = columns // kv_mine
    spread_rows = rows - swapped
    chunks = spread_rows // chunk
    units = chunk // 2
    context = n_tp * span
    scale = 1.0 / math.sqrt(size)
    f32, bf16 = jnp.float32, jnp.bfloat16

    def weight_copy(i):
        flip_x, flip_y = (i // subs) % 2, (i // subs) // 2
        column, line = lax.rem(tp, 2), tp // 2
        owner = 2 * (1 - line if flip_y else line) + (1 - column if flip_x else column)
        start = pl.multiple_of(owner * features + (i % subs) * depth, depth)
        return pltpu.make_async_copy(
            weight_hbm.at[pl.ds(start, depth), :], weight_buf.at[i % slots], weight_sem.at[i % slots]
        )

    tokens_copy = pltpu.make_async_copy(tokens_hbm, tokens_ref, load_sem.at[2])
    rope_copy = pltpu.make_async_copy(rope_hbm, rope, load_sem.at[3])
    down_copy = pltpu.make_async_copy(down_hbm, down_buf, load_sem.at[0])
    up_copy = pltpu.make_async_copy(up_hbm, up_buf, load_sem.at[1])
    tokens_copy.start()
    down_copy.start()
    for i in range(slots):
        weight_copy(i).start()
    rope_copy.start()
    up_copy.start()
    early = pl.ds(0, swapped)
    late = pl.ds(swapped, spread_rows)
    cache_copies = []
    for j in range(kv_mine):
        for which, source, near, far in (
            (0, keys_hbm, swap_keys, keys),
            (1, values_hbm, swap_values, values),
        ):
            cache_copies.append(
                pltpu.make_async_copy(
                    source.at[early, tp * kv_mine + j], near.at[j, :, 0], cache_sem.at[j, which, n_tp]
                )
            )
            for t in range(n_tp):
                cache_copies.append(
                    pltpu.make_async_copy(
                        source.at[late, t * kv_mine + j], far.at[j, :, t], cache_sem.at[j, which, t]
                    )
                )

    greetings = greet((("ad", n_ad), ("tp", n_tp)))

    index0 = lax.broadcasted_iota(jnp.int32, (rows, rows), 0)
    index1 = lax.broadcasted_iota(jnp.int32, (rows, rows), 1)
    diagonal = index0 == index1

    def to_column(row):
        return jnp.sum(jnp.where(diagonal, row, 0.0), axis=1, keepdims=True)

    def to_row(column):
        return jnp.sum(jnp.where(diagonal, column, 0.0), axis=0, keepdims=True)

    adapters = table_ref.shape[1]
    ids_column = to_column(ids_ref[...].astype(f32))
    adapter = lax.broadcasted_iota(jnp.int32, (rows, adapters), 1).astype(f32)
    slot_column = jnp.sum(
        jnp.where(ids_column == adapter, table_ref[...].astype(f32), 0.0), axis=1, keepdims=True
    )
    owner_column = jnp.floor((slot_column + 0.5) * (1.0 / held_here))
    owner_row = to_row(owner_column)
    same = owner_column == owner_row
    place_column = owner_column * cap + jnp.sum(
        jnp.where(same & (index1 < index0), 1.0, 0.0), axis=1, keepdims=True
    )
    place_row = owner_row * cap + jnp.sum(
        jnp.where(same & (index0 < index1), 1.0, 0.0), axis=0, keepdims=True
    )
    mark[...] = jnp.broadcast_to(slot_column - owner_column * held_here + 1.0, (rows, LANES)).astype(
        bf16
    )
    cell_row = lax.broadcasted_iota(jnp.int32, (cap, rows), 0)

    def pack_into(d, peer, target):
        pick = ((cell_row + peer * cap).astype(f32) == place_row).astype(bf16)

        @pl.loop(0, features // 512)
        def _(c):
            at = pl.ds(pl.multiple_of(c * 512, 512), 512)
            target[d, :, at] = jnp.dot(
                pick, tokens_ref[:, at], preferred_element_type=f32
            ).astype(bf16)

        target[d, :, pl.ds(features, LANES)] = jnp.dot(
            pick, mark[...], preferred_element_type=f32
        ).astype(bf16)

    column, line = lax.rem(tp, 2), tp // 2
    beside = [tp, 2 * line + 1 - column, 2 * (1 - line) + column, 2 * (1 - line) + 1 - column]
    halves = [pl.ds(0, rows // 2), pl.ds(rows // 2, rows // 2)]
    tok_copies = {}

    def send_tokens(e, source, h, via):
        copy = remote(
            source.at[halves[h]],
            gathered.at[e, halves[h]],
            tok_send.at[e, h],
            tok_recv.at[e, h],
            "tp",
            beside[via],
        )
        copy.start()
        tok_copies[e, h] = copy

    def forward_tokens():
        tok_copies[2, 0].wait_recv()
        send_tokens(3, gathered.at[2], 0, 1)
        tok_copies[1, 1].wait_recv()
        send_tokens(3, gathered.at[1], 1, 2)

    tokens_copy.wait()
    order = sorted(range(1, n_ad), key=lambda d: abs(d - n_ad // 2))
    row_copies = {}
    for d in order:
        peer = lax.rem(ad + d, n_ad)
        pack_into(d, peer, packed)
        if d == order[0]:
            pl.semaphore_wait(pltpu.get_barrier_semaphore(), greetings)
        copy = remote(packed.at[d], arrived.at[d], row_send.at[d], row_recv.at[d], "ad", peer)
        copy.start()
        row_copies[d] = copy
        if d == order[0]:
            for h in range(2):
                send_tokens(2, tokens_ref, h, 2)
                send_tokens(1, tokens_ref, 1 - h, 1)
    pack_into(0, ad, arrived)

    cells = lax.broadcasted_iota(jnp.int32, (rows, n_ad * cap), 1).astype(f32)
    unpack[...] = (cells == place_column).astype(bf16)
    moment = to_column(lens_ref[...].astype(f32)) - 1.0
    chosen = (lax.broadcasted_iota(jnp.int32, (rows, context), 1).astype(f32) == moment).astype(bf16)
    rope_copy.wait()
    turn = jnp.dot(chosen, rope[0], preferred_element_type=f32)
    for k in range(1, rope.shape[0]):
        turn = turn + jnp.dot(chosen, rope[k], preferred_element_type=f32)
    cosine[...] = turn[:, :size]
    sine[...] = turn[:, size:]

    swap_copies = []

    def swap(which, source, target):
        for j in range(kv_mine):
            for e in range(1, n_tp):
                peer = lax.rem(tp + e, n_tp)
                copy = remote(
                    source.at[early, peer * kv_mine + j],
                    target.at[j, :, e],
                    swap_send.at[which, j, e],
                    swap_recv.at[which, j, e],
                    "tp",
                    peer,
                )
                copy.start()
                swap_copies.append((j, copy))

    def base_chunk(e):
        if e == 1:
            tok_copies[1, 0].wait_recv()
        if e == 2:
            tok_copies[2, 1].wait_recv()
        if e == 3:
            tok_copies[3, 0].wait_recv()
            tok_copies[3, 1].wait_recv()
        block = tokens_ref if e == 0 else gathered.at[e]
        for sub in range(subs):
            i = e * subs + sub
            weight_copy(i).wait()

            @pl.loop(0, columns // 256)
            def _(c):
                at = pl.ds(pl.multiple_of(c * 256, 256), 256)
                product = jnp.dot(
                    block[:, pl.ds(sub * depth, depth)],
                    weight_buf[i % slots, :, at],
                    preferred_element_type=f32,
                )
                if i == 0:
                    acc[:, at] = product
                else:
                    acc[:, at] += product

            if i + slots < steps:
                weight_copy(i + slots).start()

    lane2 = lax.broadcasted_iota(jnp.int32, (rows2, LANES), 1)
    part_of = (lane2 // rank).astype(f32)
    lane1 = lax.broadcasted_iota(jnp.int32, (cap, LANES), 1)
    sum_copies = {}
    ret_copies = {}

    def ids_of(g):
        return (
            arrived[pl.ds(2 * g, 2), :, pl.ds(features, LANES)].reshape(rows2, LANES).astype(f32)
            - 1.0
        )

    def shrink(g):
        for d in (2 * g, 2 * g + 1):
            if d:
                row_copies[d].wait_recv()
        if g == 0:
            down_copy.wait()
        ids = ids_of(g) - part_of

        def tile(t, total):
            product = lax.dot_general(
                arrived[pl.ds(2 * g, 2), :, pl.ds(0, features)].reshape(rows2, features),
                down_buf[pl.ds(pl.multiple_of(t * 256, 256), 256), :],
                (((1,), (1,)), ((), ())),
                preferred_element_type=f32,
            )
            for k in range(per_tile):
                want = ((t * per_tile + k) * per).astype(f32)
                total = total + jnp.where(
                    ids == want, product[:, k * LANES : (k + 1) * LANES], 0.0
                )
            return total

        total = lax.fori_loop(0, tiles, tile, jnp.zeros((rows2, LANES), f32))
        total = total + pltpu.roll(total, rank, 1)
        part_send[g] = jnp.where(lane1 < rank, total[:cap], total[cap:]).astype(bf16)
        for e in range(1, n_tp):
            copy = remote(
                part_send.at[g],
                part_recv.at[g, e],
                sum_send.at[g, e],
                sum_recv.at[g, e],
                "tp",
                lax.rem(tp + e, n_tp),
            )
            copy.start()
            sum_copies[g, e] = copy

    def expand(g, j):
        if j == 0:
            if g == 0:
                up_copy.wait()
            total = part_send[g].astype(f32)
            for e in range(1, n_tp):
                sum_copies[g, e].wait_recv()
                total = total + part_recv[g, e].astype(f32)
            turned = pltpu.roll(total, rank, 1)
            both = jnp.concatenate(
                [jnp.where(lane1 < rank, total, turned), jnp.where(lane1 < rank, turned, total)],
                axis=0,
            )
            ids = ids_of(g) - part_of
            for k in range(pairs):
                spread[g, :, k * LANES : (k + 1) * LANES] = jnp.where(
                    ids == float(k * per), both, 0.0
                ).astype(bf16)

        @pl.loop(0, width // 256)
        def _(c):
            at = pl.ds(pl.multiple_of(c * 256, 256), 256)
            source = pl.ds(pl.multiple_of(j * width + c * 256, 256), 256)
            change = jnp.dot(spread[g], up_buf[:, source], preferred_element_type=f32)
            outgoing[j, pl.ds(2 * g, 2), :, at] = change.astype(bf16).reshape(2, cap, 256)

        for d in (2 * g, 2 * g + 1):
            if d:
                copy = remote(
                    outgoing.at[j, d],
                    returned.at[j, ad],
                    ret_send.at[j, d],
                    ret_recv.at[j, d],
                    "ad",
                    lax.rem(ad + n_ad - d, n_ad),
                )
                if j == 0:
                    copy.start()
                ret_copies[j, d] = copy
            else:
                returned[j, ad] = outgoing[j, 0]

    done_copies = []

    def finish(k, where, source, target):
        copy = pltpu.make_async_copy(source.at[where], target.at[where], done_sem.at[k])
        copy.start()
        done_copies.append(copy)

    sends = {}
    late_pairs = pl.ds(swapped // 2, spread_rows // 2)

    def rotate(j):
        for d in range(1, n_ad):
            ret_copies[j, d].wait_recv()
        for c in range(width // 256):
            at = pl.ds(j * width + c * 256, 256)
            delta = jnp.dot(
                unpack[...],
                returned[j, :, :, pl.ds(c * 256, 256)].reshape(n_ad * cap, 256),
                preferred_element_type=f32,
            )
            query = acc[:, at] + delta
            pieces = []
            for h in range(256 // size):
                one = query[:, h * size : (h + 1) * size]
                piece = one * cosine[...] + pltpu.roll(one, size // 2, 1) * sine[...]
                heads_f32[j, :, c * (256 // size) + h, :] = piece
                pieces.append(piece)
            out_ref[:, at] = jnp.concatenate(pieces, axis=1).astype(bf16)
        heads_bf16[j] = heads_f32[j].reshape(rows // 2, pair_rows, size).astype(bf16)
        for c in range(chunks):
            for e in range(1, n_tp):
                copy = remote(
                    heads_bf16.at[j, pl.ds(swapped // 2 + c * units, units)],
                    every.at[j, tp, pl.ds(c * units, units)],
                    q_send.at[j, c, e],
                    q_recv.at[j, c, e],
                    "tp",
                    lax.rem(tp + e, n_tp),
                )
                copy.start()
                sends[j, c, e] = copy
        every[j, tp] = heads_bf16[j, late_pairs]
        finish(j, (slice(None), pl.ds(j * width, width)), out_ref, out_hbm)

    lane = lax.broadcasted_iota(jnp.int32, (group, LANES), 1)
    half = LANES // 2

    def top_of(x, extent):
        k = extent // 2
        while k:
            flat = x.reshape(-1, LANES)
            up = pltpu.roll(flat, k, 1).reshape(x.shape)
            down = pltpu.roll(flat, LANES - k, 1).reshape(x.shape)
            x = jnp.maximum(x, jnp.where((lane // k) % 2 == 1, up, down))
            k //= 2
        return x

    def settle(j, first, count, k):
        at = pl.ds(first, count)
        for h in range(group):
            att_ref[at, j * width + h * size : j * width + (h + 1) * size] = heads_f32[
                j, at, h, :
            ].astype(bf16)
        finish(k, (at, pl.ds(j * width, width)), att_ref, att_hbm)

    near_place = lax.rem(tp + n_tp - (lane % half) // span, n_tp) * span + lane % span
    far_place = tp * span + lane % span
    seat = lane % span
    seat_of = lane // span
    ones = jnp.ones((LANES, LANES), bf16)
    belongs = (
        lax.broadcasted_iota(jnp.int32, (LANES, LANES), 0) // span
        == lax.broadcasted_iota(jnp.int32, (LANES, LANES), 1) // span
    ).astype(bf16)

    def attend_near(j):
        for k, copy in swap_copies:
            if k == j:
                copy.wait_recv()

        batch = 8

        @pl.loop(0, swapped // (2 * batch))
        def _(b):
            merged, limits = [], []
            for u in range(batch):
                p = b * batch + u
                score = lax.dot_general(
                    heads_bf16[j, p],
                    swap_keys[j, pl.ds(2 * p, 2)].reshape(LANES, size),
                    (((1,), (1,)), ((), ())),
                    preferred_element_type=f32,
                )
                merged.append(jnp.where(lane < half, score[:group], score[group:]))
                limits.append(
                    jnp.where(lane < half, lengths_ref[2 * p], lengths_ref[2 * p + 1])
                )
            valid = near_place[None] < jnp.stack(limits)
            score = jnp.where(valid, jnp.stack(merged) * scale, -1e30)
            peak = top_of(score, half)
            weight = jnp.where(valid, jnp.exp(score - peak), 0.0)
            first = jnp.where(lane < half, weight, 0.0)
            both = jnp.concatenate([first, weight - first], axis=1).astype(bf16)
            total = jnp.dot(
                both.reshape(batch * pair_rows, LANES), ones, preferred_element_type=f32
            )
            for u in range(batch):
                p = b * batch + u
                result = jnp.dot(
                    both[u],
                    swap_values[j, pl.ds(2 * p, 2)].reshape(LANES, size),
                    preferred_element_type=f32,
                )
                result = result / total[u * pair_rows : (u + 1) * pair_rows]
                heads_f32[j, pl.ds(2 * p, 2)] = result.reshape(2, group, size)

        settle(j, 0, swapped, kv_mine + j)

    unroll = 8
    outs = []

    def attend(j, c):
        for e in range(1, n_tp):
            sends[j, c, e].wait_recv()

        def some(b, held):
            peaks, totals = held
            merged, limits = [], []
            for u in range(unroll):
                p = c * units + b * unroll + u
                score = lax.dot_general(
                    jnp.concatenate([every[j, t, p] for t in range(n_tp)], axis=0),
                    keys[j, pl.ds(2 * p, 2)].reshape(LANES, size),
                    (((1,), (1,)), ((), ())),
                    preferred_element_type=f32,
                )
                one = score[:group]
                for i in range(2):
                    for t in range(n_tp):
                        at = t * pair_rows + i * group
                        one = jnp.where(seat_of == i * n_tp + t, score[at : at + group], one)
                merged.append(one)
                limits.append(
                    jnp.where(
                        lane < half, lengths_ref[swapped + 2 * p], lengths_ref[swapped + 2 * p + 1]
                    )
                )
            valid = far_place[None] < jnp.stack(limits)
            score = jnp.where(valid, jnp.stack(merged) * scale, -1e30)
            peak = top_of(score, span)
            weight = jnp.where(valid, jnp.exp(score - peak), 0.0)
            total = jnp.dot(
                weight.reshape(unroll * group, LANES).astype(bf16),
                belongs,
                preferred_element_type=f32,
            )
            for u in range(unroll):
                local = b * unroll + u
                p = c * units + local
                blocks = [
                    jnp.where(seat_of == i * n_tp + t, weight[u], 0.0)
                    for t in range(n_tp)
                    for i in range(2)
                ]
                result = jnp.dot(
                    jnp.concatenate(blocks, axis=0).astype(bf16),
                    values[j, pl.ds(2 * p, 2)].reshape(LANES, size),
                    preferred_element_type=f32,
                ).astype(bf16)
                for t in range(n_tp):
                    part[j, t, p] = result[t * pair_rows : (t + 1) * pair_rows]
                peaks = jnp.where(seat == local, peak[u], peaks)
                totals = jnp.where(seat == local, total[u * group : (u + 1) * group], totals)
            return peaks, totals

        zero = jnp.zeros((group, LANES), f32)
        peaks, totals = lax.fori_loop(0, units // unroll, some, (zero, zero))
        stat[j, c, 0] = peaks
        stat[j, c, 1] = totals
        at = pl.ds(c * units, units)
        for e in range(1, n_tp):
            peer = lax.rem(tp + e, n_tp)
            s = remote(
                stat.at[j, c], stat_in.at[j, c, e], s_send.at[j, c, e], s_recv.at[j, c, e], "tp", peer
            )
            p = remote(
                part.at[j, peer, at],
                part_in.at[j, e, at],
                p_send.at[j, c, e],
                p_recv.at[j, c, e],
                "tp",
                peer,
            )
            s.start()
            p.start()
            outs.append((j, c, s))
            outs.append((j, c, p))
        part_in[j, 0, at] = part[j, tp, at]
        stat_in[j, c, 0] = stat[j, c]

    def combine(j, c):
        for k, b, copy in outs:
            if (k, b) == (j, c):
                copy.wait_recv()
        peaks = [stat_in[j, c, e, 0] for e in range(n_tp)]
        top = functools.reduce(jnp.maximum, peaks)
        factors = [jnp.exp(s - top) for s in peaks]
        denom = sum(f * stat_in[j, c, e, 1] for e, f in enumerate(factors))
        shares = [f / denom for f in factors]

        @pl.loop(0, units // unroll)
        def _(b):
            for u in range(unroll):
                local = b * unroll + u
                p = c * units + local
                mine = tp * span + local
                result = jnp.zeros((pair_rows, size), f32)
                for e in range(n_tp):
                    share = jnp.concatenate(
                        [
                            jnp.sum(
                                jnp.where(lane == i * half + mine, shares[e], 0.0),
                                axis=1,
                                keepdims=True,
                            )
                            for i in range(2)
                        ],
                        axis=0,
                    )
                    result = result + share * part_in[j, e, p].astype(f32)
                heads_f32[j, pl.ds(swapped + 2 * p, 2)] = result.reshape(2, group, size)

        settle(j, swapped + c * chunk, chunk, 2 * kv_mine + j * chunks + c)

    base_chunk(0)
    forward_tokens()
    swap(0, keys_hbm, swap_keys)
    base_chunk(1)
    base_chunk(2)
    for copy in cache_copies:
        copy.start()
    for g in range(groups):
        shrink(g)
    swap(1, values_hbm, swap_values)
    base_chunk(3)
    for j in range(kv_mine):
        for g in range(groups):
            expand(g, j)
    for j in range(1, kv_mine):
        for d in sorted(range(1, n_ad), key=lambda d: abs(d - n_ad // 2), reverse=True):
            ret_copies[j - 1, d].wait_send()
            ret_copies[j, d].start()
    for copy in cache_copies:
        copy.wait()
    rotate(0)
    attend_near(0)
    for c in range(chunks):
        attend(0, c)
    for c in range(chunks - 1):
        combine(0, c)
    rotate(1)
    attend_near(1)
    for c in range(chunks):
        attend(1, c)
    combine(0, chunks - 1)
    for c in range(chunks):
        combine(1, c)

    for copy in list(row_copies.values()) + list(tok_copies.values()) + list(sum_copies.values()):
        copy.wait_send()
    for d in range(1, n_ad):
        ret_copies[kv_mine - 1, d].wait_send()
    for _, copy in swap_copies:
        copy.wait_send()
    for copy in list(sends.values()) + [copy for _, _, copy in outs]:
        copy.wait_send()
    for copy in done_copies:
        copy.wait()


def hand_over(first_hbm, second_hbm, out_hbm, att_hbm, held, sem):
    loads = []
    for k, source in enumerate((first_hbm, second_hbm)):
        copy = pltpu.make_async_copy(source, held.at[k], sem.at[0, k])
        copy.start()
        loads.append(copy)
    stores = []
    for k, target in enumerate((out_hbm, att_hbm)):
        loads[k].wait()
        copy = pltpu.make_async_copy(held.at[k], target, sem.at[1, k])
        copy.start()
        stores.append(copy)
    for copy in stores:
        copy.wait()


def rope_table(context, head_dim):
    half = head_dim // 2
    freq = np.exp(np.arange(half, dtype=np.float64) * (-2.0 * math.log(500000.0) / head_dim))
    freq = freq.astype(np.float32).astype(np.float64)
    angle = (np.arange(context, dtype=np.float64)[:, None] * freq[None, :]).astype(np.float32)
    cosine, sine = np.cos(angle.astype(np.float64)), np.sin(angle.astype(np.float64))
    rest = np.concatenate([cosine, cosine, -sine, sine], axis=1).astype(np.float32)
    terms = []
    for _ in range(3):
        term = rest.astype(jnp.bfloat16)
        terms.append(term)
        rest = rest - term.astype(np.float32)
    return np.stack(terms)


def fused_device(
    tokens,
    query_weight,
    adapter_down_weight,
    adapter_up_weight,
    row_adapter_index,
    adapter_table_slot,
    lengths,
    cached_key_rows,
    cached_value_rows,
):
    rows, features = tokens.shape
    columns = query_weight.shape[1]
    n_ad = lax.axis_size("ad")
    n_tp = lax.axis_size("tp")
    held = adapter_down_weight.shape[0]
    rank = adapter_down_weight.shape[2]
    _, kv_heads, span, head_dim = cached_key_rows.shape
    cap = -(-(384 // n_ad) // 16) * 16

    depth = 1024
    slot_count = 4
    swapped = SWAPPED
    chunk = CHUNK
    heads = columns // head_dim
    spread_rows = rows - swapped
    chunks = spread_rows // chunk
    kv_mine = kv_heads // n_tp
    group = heads // kv_mine
    pairs = rows // 2
    spread_pairs = spread_rows // 2
    width = columns // kv_mine
    vmem = pl.BlockSpec(memory_space=pltpu.VMEM)
    smem = pl.BlockSpec(memory_space=pltpu.SMEM)
    anywhere = pl.BlockSpec(memory_space=pl.ANY)
    bf16, f32 = jnp.bfloat16, jnp.float32
    dma = pltpu.SemaphoreType.DMA
    groups = n_ad // 2
    rope = rope_table(n_tp * span, head_dim)
    results = pl.pallas_call(
        functools.partial(step_kernel, n_ad, n_tp, cap, rank, swapped, chunk),
        out_shape=(jax.ShapeDtypeStruct((rows, columns), bf16),) * 2,
        in_specs=[vmem] * 3 + [smem] + [anywhere] * 7,
        out_specs=(anywhere, anywhere),
        scratch_shapes=[
            pltpu.VMEM((rows, features), bf16),
            pltpu.VMEM(rope.shape, bf16),
            pltpu.VMEM((rows, LANES), bf16),
            pltpu.VMEM((rows, n_ad * cap), bf16),
            pltpu.VMEM((rows, head_dim), f32),
            pltpu.VMEM((rows, head_dim), f32),
            pltpu.VMEM((n_ad, cap, features + LANES), bf16),
            pltpu.VMEM((n_tp, rows, features), bf16),
            pltpu.VMEM((n_ad, cap, features + LANES), bf16),
            pltpu.VMEM((groups, 2 * cap, held * rank), bf16),
            pltpu.VMEM((kv_mine, n_ad, cap, width), bf16),
            pltpu.VMEM((kv_mine, n_ad, cap, width), bf16),
            pltpu.VMEM((groups, cap, LANES), bf16),
            pltpu.VMEM((groups, n_tp, cap, LANES), bf16),
            pltpu.VMEM((rows, columns), f32),
            pltpu.VMEM((slot_count, depth, columns), bf16),
            pltpu.VMEM((held * rank, features), bf16),
            pltpu.VMEM((held * rank, columns), bf16),
            pltpu.VMEM((rows, columns), bf16),
            pltpu.VMEM((rows, columns), bf16),
            pltpu.VMEM((kv_mine, rows, group, head_dim), f32),
            pltpu.VMEM((kv_mine, pairs, 2 * group, head_dim), bf16),
            pltpu.VMEM((kv_mine, swapped, n_tp, span, head_dim), bf16),
            pltpu.VMEM((kv_mine, swapped, n_tp, span, head_dim), bf16),
            pltpu.VMEM((kv_mine, n_tp, spread_pairs, 2 * group, head_dim), bf16),
            pltpu.VMEM((kv_mine, spread_rows, n_tp, span, head_dim), bf16),
            pltpu.VMEM((kv_mine, spread_rows, n_tp, span, head_dim), bf16),
            pltpu.VMEM((kv_mine, n_tp, spread_pairs, 2 * group, head_dim), bf16),
            pltpu.VMEM((kv_mine, chunks, 2, group, LANES), f32),
            pltpu.VMEM((kv_mine, n_tp, spread_pairs, 2 * group, head_dim), bf16),
            pltpu.VMEM((kv_mine, chunks, n_tp, 2, group, LANES), f32),
            dma((slot_count,)),
            dma((4,)),
            dma((kv_mine, 2, n_tp + 1)),
            dma((2 * kv_mine + kv_mine * chunks,)),
            dma((n_tp, 2)),
            dma((n_tp, 2)),
            dma((n_ad,)),
            dma((n_ad,)),
            dma((groups, n_tp)),
            dma((groups, n_tp)),
            dma((kv_mine, n_ad)),
            dma((kv_mine, n_ad)),
            dma((2, kv_mine, n_tp)),
            dma((2, kv_mine, n_tp)),
            dma((kv_mine, chunks, n_tp)),
            dma((kv_mine, chunks, n_tp)),
            dma((kv_mine, chunks, n_tp)),
            dma((kv_mine, chunks, n_tp)),
            dma((kv_mine, chunks, n_tp)),
            dma((kv_mine, chunks, n_tp)),
        ],
        compiler_params=pltpu.CompilerParams(
            collective_id=0, has_side_effects=True, vmem_limit_bytes=60 * 1024 * 1024
        ),
        name="step",
    )(
        row_adapter_index[None, :],
        adapter_table_slot[None, :],
        lengths[None, :],
        lengths,
        tokens,
        jnp.asarray(rope),
        query_weight,
        adapter_down_weight.transpose(0, 2, 1).reshape(held * rank, features),
        adapter_up_weight.reshape(held * rank, columns),
        cached_key_rows,
        cached_value_rows,
    )
    return pl.pallas_call(
        hand_over,
        out_shape=(jax.ShapeDtypeStruct((rows, columns), bf16),) * 2,
        in_specs=[anywhere] * 2,
        out_specs=(anywhere, anywhere),
        scratch_shapes=[pltpu.VMEM((2, rows, columns), bf16), dma((2, 2))],
        name="hand_over",
    )(*results)


def rotate(query, lengths):
    head_dim = query.shape[-1]
    half = head_dim // 2
    freq = jnp.exp(jnp.arange(half, dtype=jnp.float32) * (-2.0 * math.log(500000.0) / head_dim))
    angle = (lengths - 1).astype(jnp.float32)[:, None, None] * freq[None, None, :]
    cosine = jnp.cos(angle)
    sine = jnp.sin(angle)
    first = query[..., :half]
    second = query[..., half:]
    return jnp.concatenate(
        [first * cosine - second * sine, second * cosine + first * sine], axis=-1
    )


def lookup(ids, adapter_table_slot):
    table = jnp.arange(adapter_table_slot.shape[0], dtype=jnp.int32)
    return jnp.sum(
        jnp.where(ids[:, None] == table[None, :], adapter_table_slot[None, :], 0), axis=1
    )


def shrink_rows(input_rows, local_partial, adapter_down_weight):
    adapter_row_count = adapter_down_weight.shape[0]
    select_rows = (
        local_partial[:, None] == jnp.arange(adapter_row_count, dtype=jnp.int32)[None, :]
    ).astype(jnp.float32)
    update_terms = jnp.einsum(
        "nt,vtm->nvm", input_rows, adapter_down_weight, preferred_element_type=jnp.float32
    )
    return (select_rows, jnp.sum(update_terms * select_rows[:, :, None], axis=1))


def expand_rows(select_rows, reduced_rows, adapter_up_weight):
    spread_rows = (select_rows[:, :, None] * reduced_rows.astype(jnp.float32)[:, None, :]).astype(
        jnp.bfloat16
    )
    return jnp.einsum(
        "pow,owu->pu", spread_rows, adapter_up_weight, preferred_element_type=jnp.float32
    ).astype(jnp.bfloat16)


def per_device(
    tokens,
    query_weight,
    adapter_down_weight,
    adapter_up_weight,
    row_adapter_index,
    adapter_table_slot,
    lengths,
    cached_key_rows,
    cached_value_rows,
):
    rows = tokens.shape[0]
    columns = query_weight.shape[1]
    tp_count = lax.axis_size("tp")
    owner_partials = adapter_down_weight.shape[0]
    base = jnp.dot(
        lax.all_gather(tokens, "tp", axis=1, tiled=True),
        query_weight,
        preferred_element_type=jnp.float32,
    )
    combined_output, every_id = (
        lax.all_gather(tokens, "ad", axis=0, tiled=True),
        lax.all_gather(row_adapter_index, "ad", axis=0, tiled=True),
    )
    slots = lookup(every_id, adapter_table_slot)
    mine = slots // owner_partials == lax.axis_index("ad")
    local_partial = jnp.where(mine, slots % owner_partials, -1)
    select_rows, partial_value_sum = shrink_rows(
        combined_output, local_partial, adapter_down_weight
    )
    reduced_rows = lax.psum(partial_value_sum, "tp").astype(jnp.bfloat16)
    lowrank_change = expand_rows(select_rows, reduced_rows, adapter_up_weight)
    delta = lax.psum_scatter(
        lowrank_change.astype(jnp.float32).astype(jnp.bfloat16),
        "ad",
        scatter_dimension=0,
        tiled=True,
    ).astype(jnp.float32)
    head_dim = cached_key_rows.shape[3]
    query = (base + delta).reshape(rows, columns // head_dim, head_dim)
    queries = rotate(query, lengths).reshape(rows, columns).astype(jnp.bfloat16)
    every_head = lax.all_gather(queries, "tp", axis=1, tiled=True)
    kv_heads = cached_key_rows.shape[1]
    span = cached_key_rows.shape[2]
    grouped = every_head.reshape(rows, kv_heads, -1, head_dim)
    scores = jnp.einsum(
        "rkgd,rkpd->rkgp", grouped, cached_key_rows, preferred_element_type=jnp.float32
    ) * (1.0 / math.sqrt(head_dim))
    position = lax.axis_index("tp") * span + jnp.arange(span, dtype=jnp.int32)
    valid = (position[None, :] < lengths[:, None])[:, None, None, :]
    scores = jnp.where(valid, scores, -1e30)
    peak = jnp.max(scores, axis=-1)
    weights = jnp.where(valid, jnp.exp(scores - peak[..., None]), 0.0)
    total = jnp.sum(weights, axis=-1)
    partial_out = jnp.einsum(
        "rkgp,rkpd->rkgd",
        weights.astype(jnp.bfloat16),
        cached_value_rows,
        preferred_element_type=jnp.float32,
    ).astype(jnp.bfloat16)
    peaks, totals = (
        lax.all_to_all(
            peak.reshape(rows, tp_count, -1), "tp", split_axis=1, concat_axis=1, tiled=True
        ),
        lax.all_to_all(
            total.reshape(rows, tp_count, -1), "tp", split_axis=1, concat_axis=1, tiled=True
        ),
    )
    partials = lax.all_to_all(
        partial_out.reshape(rows, tp_count, -1), "tp", split_axis=1, concat_axis=1, tiled=True
    )
    highest = jnp.max(peaks, axis=1, keepdims=True)
    factor = jnp.exp(peaks - highest)
    numer = jnp.sum(
        factor[..., None] * partials.reshape(rows, tp_count, -1, head_dim).astype(jnp.float32),
        axis=1,
    )
    denom = jnp.sum(factor * totals, axis=1)
    attended = (numer / denom[..., None]).reshape(rows, columns).astype(jnp.bfloat16)
    return (queries, attended)


def solution(mesh):
    fits = mesh.shape["tp"] == 4 and mesh.shape["ad"] == 8
    return jax.shard_map(
        fused_device if fits else per_device,
        mesh=mesh,
        in_specs=(
            P("ad", "tp"),
            P(None, "tp"),
            P("ad", "tp", None),
            P("ad", None, "tp"),
            P("ad"),
            P(),
            P("ad"),
            P("ad", None, "tp", None),
            P("ad", None, "tp", None),
        ),
        out_specs=(P("ad", "tp"), P("ad", "tp")),
        check_vma=False,
    )
```

```python
import functools
import math

import jax
import jax.numpy as jnp
import numpy as np
from jax import lax
from jax.experimental import pallas as pl
from jax.experimental.pallas import tpu as pltpu
from jax.sharding import PartitionSpec as P

MESH = pl.DeviceIdType.MESH
LANES = 128
SWAPPED = 64
CHUNK = 32


def remote(src, dst, send_sem, recv_sem, axis, peer):
    return pltpu.make_async_remote_copy(
        src_ref=src,
        dst_ref=dst,
        send_sem=send_sem,
        recv_sem=recv_sem,
        device_id={axis: peer},
        device_id_type=MESH,
    )


def greet(counts):
    barrier = pltpu.get_barrier_semaphore()
    total = 0
    for axis, count in counts:
        me = lax.axis_index(axis)
        for d in range(1, count):
            pl.semaphore_signal(
                barrier, inc=1, device_id={axis: lax.rem(me + d, count)}, device_id_type=MESH
            )
            total += 1
    return total


def step_kernel(
    n_ad,
    n_tp,
    cap,
    rank,
    swapped,
    chunk,
    ids_ref,
    table_ref,
    lens_ref,
    lengths_ref,
    tokens_hbm,
    rope_hbm,
    weight_hbm,
    down_hbm,
    up_hbm,
    keys_hbm,
    values_hbm,
    out_hbm,
    att_hbm,
    tokens_ref,
    rope,
    mark,
    unpack,
    cosine,
    sine,
    packed,
    gathered,
    arrived,
    spread,
    outgoing,
    returned,
    part_send,
    part_recv,
    acc,
    weight_buf,
    down_buf,
    up_buf,
    out_ref,
    att_ref,
    heads_f32,
    heads_bf16,
    swap_keys,
    swap_values,
    every,
    keys,
    values,
    part,
    stat,
    part_in,
    stat_in,
    weight_sem,
    load_sem,
    cache_sem,
    done_sem,
    tok_send,
    tok_recv,
    row_send,
    row_recv,
    sum_send,
    sum_recv,
    ret_send,
    ret_recv,
    swap_send,
    swap_recv,
    q_send,
    q_recv,
    p_send,
    p_recv,
    s_send,
    s_recv,
):
    ad = lax.axis_index("ad")
    tp = lax.axis_index("tp")
    rows, features = tokens_ref.shape
    columns = out_ref.shape[1]
    depth = weight_buf.shape[1]
    slots = weight_buf.shape[0]
    subs = features // depth
    steps = n_tp * subs
    per = LANES // rank
    held_here = down_buf.shape[0] // rank
    pairs = down_buf.shape[0] // LANES
    tiles = down_buf.shape[0] // 256
    per_tile = 256 // LANES
    groups = n_ad // 2
    rows2 = 2 * cap
    kv_mine, _, pair_rows, size = heads_bf16.shape
    group = pair_rows // 2
    span = keys_hbm.shape[2]
    width = columns // kv_mine
    spread_rows = rows - swapped
    chunks = spread_rows // chunk
    units = chunk // 2
    context = n_tp * span
    scale = 1.0 / math.sqrt(size)
    f32, bf16 = jnp.float32, jnp.bfloat16

    def weight_copy(i):
        flip_x, flip_y = (i // subs) % 2, (i // subs) // 2
        column, line = lax.rem(tp, 2), tp // 2
        owner = 2 * (1 - line if flip_y else line) + (1 - column if flip_x else column)
        start = pl.multiple_of(owner * features + (i % subs) * depth, depth)
        return pltpu.make_async_copy(
            weight_hbm.at[pl.ds(start, depth), :], weight_buf.at[i % slots], weight_sem.at[i % slots]
        )

    tokens_copy = pltpu.make_async_copy(tokens_hbm, tokens_ref, load_sem.at[2])
    rope_copy = pltpu.make_async_copy(rope_hbm, rope, load_sem.at[3])
    down_copy = pltpu.make_async_copy(down_hbm, down_buf, load_sem.at[0])
    up_copy = pltpu.make_async_copy(up_hbm, up_buf, load_sem.at[1])
    tokens_copy.start()
    down_copy.start()
    for i in range(slots):
        weight_copy(i).start()
    rope_copy.start()
    up_copy.start()
    early = pl.ds(0, swapped)
    late = pl.ds(swapped, spread_rows)
    cache_copies = []
    for j in range(kv_mine):
        for which, source, near, far in (
            (0, keys_hbm, swap_keys, keys),
            (1, values_hbm, swap_values, values),
        ):
            cache_copies.append(
                pltpu.make_async_copy(
                    source.at[early, tp * kv_mine + j], near.at[j, :, 0], cache_sem.at[j, which, n_tp]
                )
            )
            for t in range(n_tp):
                cache_copies.append(
                    pltpu.make_async_copy(
                        source.at[late, t * kv_mine + j], far.at[j, :, t], cache_sem.at[j, which, t]
                    )
                )

    greetings = greet((("ad", n_ad), ("tp", n_tp)))

    index0 = lax.broadcasted_iota(jnp.int32, (rows, rows), 0)
    index1 = lax.broadcasted_iota(jnp.int32, (rows, rows), 1)
    diagonal = index0 == index1

    def to_column(row):
        return jnp.sum(jnp.where(diagonal, row, 0.0), axis=1, keepdims=True)

    def to_row(column):
        return jnp.sum(jnp.where(diagonal, column, 0.0), axis=0, keepdims=True)

    adapters = table_ref.shape[1]
    ids_column = to_column(ids_ref[...].astype(f32))
    adapter = lax.broadcasted_iota(jnp.int32, (rows, adapters), 1).astype(f32)
    slot_column = jnp.sum(
        jnp.where(ids_column == adapter, table_ref[...].astype(f32), 0.0), axis=1, keepdims=True
    )
    owner_column = jnp.floor((slot_column + 0.5) * (1.0 / held_here))
    owner_row = to_row(owner_column)
    same = owner_column == owner_row
    place_column = owner_column * cap + jnp.sum(
        jnp.where(same & (index1 < index0), 1.0, 0.0), axis=1, keepdims=True
    )
    place_row = owner_row * cap + jnp.sum(
        jnp.where(same & (index0 < index1), 1.0, 0.0), axis=0, keepdims=True
    )
    mark[...] = jnp.broadcast_to(slot_column - owner_column * held_here + 1.0, (rows, LANES)).astype(
        bf16
    )
    cell_row = lax.broadcasted_iota(jnp.int32, (cap, rows), 0)

    def pack_into(d, peer, target):
        pick = ((cell_row + peer * cap).astype(f32) == place_row).astype(bf16)

        @pl.loop(0, features // 512)
        def _(c):
            at = pl.ds(pl.multiple_of(c * 512, 512), 512)
            target[d, :, at] = jnp.dot(
                pick, tokens_ref[:, at], preferred_element_type=f32
            ).astype(bf16)

        target[d, :, pl.ds(features, LANES)] = jnp.dot(
            pick, mark[...], preferred_element_type=f32
        ).astype(bf16)

    column, line = lax.rem(tp, 2), tp // 2
    beside = [tp, 2 * line + 1 - column, 2 * (1 - line) + column, 2 * (1 - line) + 1 - column]
    halves = [pl.ds(0, rows // 2), pl.ds(rows // 2, rows // 2)]
    tok_copies = {}

    def send_tokens(e, source, h, via):
        copy = remote(
            source.at[halves[h]],
            gathered.at[e, halves[h]],
            tok_send.at[e, h],
            tok_recv.at[e, h],
            "tp",
            beside[via],
        )
        copy.start()
        tok_copies[e, h] = copy

    def forward_tokens():
        tok_copies[2, 0].wait_recv()
        send_tokens(3, gathered.at[2], 0, 1)
        tok_copies[1, 1].wait_recv()
        send_tokens(3, gathered.at[1], 1, 2)

    tokens_copy.wait()
    order = sorted(range(1, n_ad), key=lambda d: abs(d - n_ad // 2))
    row_copies = {}
    for d in order:
        peer = lax.rem(ad + d, n_ad)
        pack_into(d, peer, packed)
        if d == order[0]:
            pl.semaphore_wait(pltpu.get_barrier_semaphore(), greetings)
        copy = remote(packed.at[d], arrived.at[d], row_send.at[d], row_recv.at[d], "ad", peer)
        copy.start()
        row_copies[d] = copy
        if d == order[0]:
            for h in range(2):
                send_tokens(2, tokens_ref, h, 2)
                send_tokens(1, tokens_ref, 1 - h, 1)
    pack_into(0, ad, arrived)

    cells = lax.broadcasted_iota(jnp.int32, (rows, n_ad * cap), 1).astype(f32)
    unpack[...] = (cells == place_column).astype(bf16)
    moment = to_column(lens_ref[...].astype(f32)) - 1.0
    chosen = (lax.broadcasted_iota(jnp.int32, (rows, context), 1).astype(f32) == moment).astype(bf16)
    rope_copy.wait()
    turn = jnp.dot(chosen, rope[0], preferred_element_type=f32)
    for k in range(1, rope.shape[0]):
        turn = turn + jnp.dot(chosen, rope[k], preferred_element_type=f32)
    cosine[...] = turn[:, :size]
    sine[...] = turn[:, size:]

    swap_copies = []

    def swap(which, source, target):
        for j in range(kv_mine):
            for e in range(1, n_tp):
                peer = lax.rem(tp + e, n_tp)
                copy = remote(
                    source.at[early, peer * kv_mine + j],
                    target.at[j, :, e],
                    swap_send.at[which, j, e],
                    swap_recv.at[which, j, e],
                    "tp",
                    peer,
                )
                copy.start()
                swap_copies.append((j, copy))

    def base_chunk(e):
        if e == 1:
            tok_copies[1, 0].wait_recv()
        if e == 2:
            tok_copies[2, 1].wait_recv()
        if e == 3:
            tok_copies[3, 0].wait_recv()
            tok_copies[3, 1].wait_recv()
        block = tokens_ref if e == 0 else gathered.at[e]
        for sub in range(subs):
            i = e * subs + sub
            weight_copy(i).wait()

            @pl.loop(0, columns // 256)
            def _(c):
                at = pl.ds(pl.multiple_of(c * 256, 256), 256)
                product = jnp.dot(
                    block[:, pl.ds(sub * depth, depth)],
                    weight_buf[i % slots, :, at],
                    preferred_element_type=f32,
                )
                if i == 0:
                    acc[:, at] = product
                else:
                    acc[:, at] += product

            if i + slots < steps:
                weight_copy(i + slots).start()

    lane2 = lax.broadcasted_iota(jnp.int32, (rows2, LANES), 1)
    part_of = (lane2 // rank).astype(f32)
    lane1 = lax.broadcasted_iota(jnp.int32, (cap, LANES), 1)
    sum_copies = {}
    ret_copies = {}

    def ids_of(g):
        return (
            arrived[pl.ds(2 * g, 2), :, pl.ds(features, LANES)].reshape(rows2, LANES).astype(f32)
            - 1.0
        )

    def shrink(g):
        for d in (2 * g, 2 * g + 1):
            if d:
                row_copies[d].wait_recv()
        if g == 0:
            down_copy.wait()
        ids = ids_of(g) - part_of

        def tile(t, total):
            product = lax.dot_general(
                arrived[pl.ds(2 * g, 2), :, pl.ds(0, features)].reshape(rows2, features),
                down_buf[pl.ds(pl.multiple_of(t * 256, 256), 256), :],
                (((1,), (1,)), ((), ())),
                preferred_element_type=f32,
            )
            for k in range(per_tile):
                want = ((t * per_tile + k) * per).astype(f32)
                total = total + jnp.where(
                    ids == want, product[:, k * LANES : (k + 1) * LANES], 0.0
                )
            return total

        total = lax.fori_loop(0, tiles, tile, jnp.zeros((rows2, LANES), f32))
        total = total + pltpu.roll(total, rank, 1)
        part_send[g] = jnp.where(lane1 < rank, total[:cap], total[cap:]).astype(bf16)
        for e in range(1, n_tp):
            copy = remote(
                part_send.at[g],
                part_recv.at[g, e],
                sum_send.at[g, e],
                sum_recv.at[g, e],
                "tp",
                lax.rem(tp + e, n_tp),
            )
            copy.start()
            sum_copies[g, e] = copy

    def expand(g, j):
        if j == 0:
            if g == 0:
                up_copy.wait()
            total = part_send[g].astype(f32)
            for e in range(1, n_tp):
                sum_copies[g, e].wait_recv()
                total = total + part_recv[g, e].astype(f32)
            turned = pltpu.roll(total, rank, 1)
            both = jnp.concatenate(
                [jnp.where(lane1 < rank, total, turned), jnp.where(lane1 < rank, turned, total)],
                axis=0,
            )
            ids = ids_of(g) - part_of
            for k in range(pairs):
                spread[g, :, k * LANES : (k + 1) * LANES] = jnp.where(
                    ids == float(k * per), both, 0.0
                ).astype(bf16)

        @pl.loop(0, width // 256)
        def _(c):
            at = pl.ds(pl.multiple_of(c * 256, 256), 256)
            source = pl.ds(pl.multiple_of(j * width + c * 256, 256), 256)
            change = jnp.dot(spread[g], up_buf[:, source], preferred_element_type=f32)
            outgoing[j, pl.ds(2 * g, 2), :, at] = change.astype(bf16).reshape(2, cap, 256)

        for d in (2 * g, 2 * g + 1):
            if d:
                copy = remote(
                    outgoing.at[j, d],
                    returned.at[j, ad],
                    ret_send.at[j, d],
                    ret_recv.at[j, d],
                    "ad",
                    lax.rem(ad + n_ad - d, n_ad),
                )
                if j == 0:
                    copy.start()
                ret_copies[j, d] = copy
            else:
                returned[j, ad] = outgoing[j, 0]

    done_copies = []

    def finish(k, where, source, target):
        copy = pltpu.make_async_copy(source.at[where], target.at[where], done_sem.at[k])
        copy.start()
        done_copies.append(copy)

    sends = {}
    late_pairs = pl.ds(swapped // 2, spread_rows // 2)

    def rotate(j):
        for d in range(1, n_ad):
            ret_copies[j, d].wait_recv()
        for c in range(width // 256):
            at = pl.ds(j * width + c * 256, 256)
            delta = jnp.dot(
                unpack[...],
                returned[j, :, :, pl.ds(c * 256, 256)].reshape(n_ad * cap, 256),
                preferred_element_type=f32,
            )
            query = acc[:, at] + delta
            pieces = []
            for h in range(256 // size):
                one = query[:, h * size : (h + 1) * size]
                piece = one * cosine[...] + pltpu.roll(one, size // 2, 1) * sine[...]
                heads_f32[j, :, c * (256 // size) + h, :] = piece
                pieces.append(piece)
            out_ref[:, at] = jnp.concatenate(pieces, axis=1).astype(bf16)
        heads_bf16[j] = heads_f32[j].reshape(rows // 2, pair_rows, size).astype(bf16)
        for c in range(chunks):
            for e in range(1, n_tp):
                copy = remote(
                    heads_bf16.at[j, pl.ds(swapped // 2 + c * units, units)],
                    every.at[j, tp, pl.ds(c * units, units)],
                    q_send.at[j, c, e],
                    q_recv.at[j, c, e],
                    "tp",
                    lax.rem(tp + e, n_tp),
                )
                copy.start()
                sends[j, c, e] = copy
        every[j, tp] = heads_bf16[j, late_pairs]
        finish(j, (slice(None), pl.ds(j * width, width)), out_ref, out_hbm)

    lane = lax.broadcasted_iota(jnp.int32, (group, LANES), 1)
    half = LANES // 2

    def top_of(x, extent):
        k = extent // 2
        while k:
            flat = x.reshape(-1, LANES)
            up = pltpu.roll(flat, k, 1).reshape(x.shape)
            down = pltpu.roll(flat, LANES - k, 1).reshape(x.shape)
            x = jnp.maximum(x, jnp.where((lane // k) % 2 == 1, up, down))
            k //= 2
        return x

    def settle(j, first, count, k):
        at = pl.ds(first, count)
        for h in range(group):
            att_ref[at, j * width + h * size : j * width + (h + 1) * size] = heads_f32[
                j, at, h, :
            ].astype(bf16)
        finish(k, (at, pl.ds(j * width, width)), att_ref, att_hbm)

    near_place = lax.rem(tp + n_tp - (lane % half) // span, n_tp) * span + lane % span
    far_place = tp * span + lane % span
    seat = lane % span
    seat_of = lane // span
    ones = jnp.ones((LANES, LANES), bf16)
    belongs = (
        lax.broadcasted_iota(jnp.int32, (LANES, LANES), 0) // span
        == lax.broadcasted_iota(jnp.int32, (LANES, LANES), 1) // span
    ).astype(bf16)

    def attend_near(j):
        for k, copy in swap_copies:
            if k == j:
                copy.wait_recv()

        batch = 8

        @pl.loop(0, swapped // (2 * batch))
        def _(b):
            merged, limits = [], []
            for u in range(batch):
                p = b * batch + u
                score = lax.dot_general(
                    heads_bf16[j, p],
                    swap_keys[j, pl.ds(2 * p, 2)].reshape(LANES, size),
                    (((1,), (1,)), ((), ())),
                    preferred_element_type=f32,
                )
                merged.append(jnp.where(lane < half, score[:group], score[group:]))
                limits.append(
                    jnp.where(lane < half, lengths_ref[2 * p], lengths_ref[2 * p + 1])
                )
            valid = near_place[None] < jnp.stack(limits)
            score = jnp.where(valid, jnp.stack(merged) * scale, -1e30)
            peak = top_of(score, half)
            weight = jnp.where(valid, jnp.exp(score - peak), 0.0)
            first = jnp.where(lane < half, weight, 0.0)
            both = jnp.concatenate([first, weight - first], axis=1).astype(bf16)
            total = jnp.dot(
                both.reshape(batch * pair_rows, LANES), ones, preferred_element_type=f32
            )
            for u in range(batch):
                p = b * batch + u
                result = jnp.dot(
                    both[u],
                    swap_values[j, pl.ds(2 * p, 2)].reshape(LANES, size),
                    preferred_element_type=f32,
                )
                result = result / total[u * pair_rows : (u + 1) * pair_rows]
                heads_f32[j, pl.ds(2 * p, 2)] = result.reshape(2, group, size)

        settle(j, 0, swapped, kv_mine + j)

    unroll = 16
    outs = []

    def attend(j, c):
        for e in range(1, n_tp):
            sends[j, c, e].wait_recv()

        def some(b, held):
            peaks, totals = held
            merged, limits = [], []
            for u in range(unroll):
                p = c * units + b * unroll + u
                score = lax.dot_general(
                    jnp.concatenate([every[j, t, p] for t in range(n_tp)], axis=0),
                    keys[j, pl.ds(2 * p, 2)].reshape(LANES, size),
                    (((1,), (1,)), ((), ())),
                    preferred_element_type=f32,
                )
                one = score[:group]
                for i in range(2):
                    for t in range(n_tp):
                        at = t * pair_rows + i * group
                        one = jnp.where(seat_of == i * n_tp + t, score[at : at + group], one)
                merged.append(one)
                limits.append(
                    jnp.where(
                        lane < half, lengths_ref[swapped + 2 * p], lengths_ref[swapped + 2 * p + 1]
                    )
                )
            valid = far_place[None] < jnp.stack(limits)
            score = jnp.where(valid, jnp.stack(merged) * scale, -1e30)
            peak = top_of(score, span)
            weight = jnp.where(valid, jnp.exp(score - peak), 0.0)
            total = jnp.dot(
                weight.reshape(unroll * group, LANES).astype(bf16),
                belongs,
                preferred_element_type=f32,
            )
            for u in range(unroll):
                local = b * unroll + u
                p = c * units + local
                blocks = [
                    jnp.where(seat_of == i * n_tp + t, weight[u], 0.0)
                    for t in range(n_tp)
                    for i in range(2)
                ]
                result = jnp.dot(
                    jnp.concatenate(blocks, axis=0).astype(bf16),
                    values[j, pl.ds(2 * p, 2)].reshape(LANES, size),
                    preferred_element_type=f32,
                ).astype(bf16)
                for t in range(n_tp):
                    part[j, t, p] = result[t * pair_rows : (t + 1) * pair_rows]
                peaks = jnp.where(seat == local, peak[u], peaks)
                totals = jnp.where(seat == local, total[u * group : (u + 1) * group], totals)
            return peaks, totals

        zero = jnp.zeros((group, LANES), f32)
        peaks, totals = lax.fori_loop(0, units // unroll, some, (zero, zero))
        stat[j, c, 0] = peaks
        stat[j, c, 1] = totals
        at = pl.ds(c * units, units)
        for e in range(1, n_tp):
            peer = lax.rem(tp + e, n_tp)
            s = remote(
                stat.at[j, c], stat_in.at[j, c, e], s_send.at[j, c, e], s_recv.at[j, c, e], "tp", peer
            )
            p = remote(
                part.at[j, peer, at],
                part_in.at[j, e, at],
                p_send.at[j, c, e],
                p_recv.at[j, c, e],
                "tp",
                peer,
            )
            s.start()
            p.start()
            outs.append((j, c, s))
            outs.append((j, c, p))
        part_in[j, 0, at] = part[j, tp, at]
        stat_in[j, c, 0] = stat[j, c]

    def combine(j, c):
        for k, b, copy in outs:
            if (k, b) == (j, c):
                copy.wait_recv()
        peaks = [stat_in[j, c, e, 0] for e in range(n_tp)]
        top = functools.reduce(jnp.maximum, peaks)
        factors = [jnp.exp(s - top) for s in peaks]
        denom = sum(f * stat_in[j, c, e, 1] for e, f in enumerate(factors))
        shares = [f / denom for f in factors]

        @pl.loop(0, units // unroll)
        def _(b):
            for u in range(unroll):
                local = b * unroll + u
                p = c * units + local
                mine = tp * span + local
                result = jnp.zeros((pair_rows, size), f32)
                for e in range(n_tp):
                    share = jnp.concatenate(
                        [
                            jnp.sum(
                                jnp.where(lane == i * half + mine, shares[e], 0.0),
                                axis=1,
                                keepdims=True,
                            )
                            for i in range(2)
                        ],
                        axis=0,
                    )
                    result = result + share * part_in[j, e, p].astype(f32)
                heads_f32[j, pl.ds(swapped + 2 * p, 2)] = result.reshape(2, group, size)

        settle(j, swapped + c * chunk, chunk, 2 * kv_mine + j * chunks + c)

    base_chunk(0)
    forward_tokens()
    swap(0, keys_hbm, swap_keys)
    base_chunk(1)
    base_chunk(2)
    for copy in cache_copies:
        copy.start()
    for g in range(groups):
        shrink(g)
    swap(1, values_hbm, swap_values)
    base_chunk(3)
    for j in range(kv_mine):
        for g in range(groups):
            expand(g, j)
    for j in range(1, kv_mine):
        for d in sorted(range(1, n_ad), key=lambda d: abs(d - n_ad // 2), reverse=True):
            ret_copies[j - 1, d].wait_send()
            ret_copies[j, d].start()
    for copy in cache_copies:
        copy.wait()
    rotate(0)
    attend_near(0)
    for c in range(chunks):
        attend(0, c)
    for c in range(chunks - 1):
        combine(0, c)
    rotate(1)
    attend_near(1)
    for c in range(chunks):
        attend(1, c)
    combine(0, chunks - 1)
    for c in range(chunks):
        combine(1, c)

    for copy in list(row_copies.values()) + list(tok_copies.values()) + list(sum_copies.values()):
        copy.wait_send()
    for d in range(1, n_ad):
        ret_copies[kv_mine - 1, d].wait_send()
    for _, copy in swap_copies:
        copy.wait_send()
    for copy in list(sends.values()) + [copy for _, _, copy in outs]:
        copy.wait_send()
    for copy in done_copies:
        copy.wait()


def hand_over(first_hbm, second_hbm, out_hbm, att_hbm, held, sem):
    loads = []
    for k, source in enumerate((first_hbm, second_hbm)):
        copy = pltpu.make_async_copy(source, held.at[k], sem.at[0, k])
        copy.start()
        loads.append(copy)
    stores = []
    for k, target in enumerate((out_hbm, att_hbm)):
        loads[k].wait()
        copy = pltpu.make_async_copy(held.at[k], target, sem.at[1, k])
        copy.start()
        stores.append(copy)
    for copy in stores:
        copy.wait()


def rope_table(context, head_dim):
    half = head_dim // 2
    freq = np.exp(np.arange(half, dtype=np.float64) * (-2.0 * math.log(500000.0) / head_dim))
    freq = freq.astype(np.float32).astype(np.float64)
    angle = (np.arange(context, dtype=np.float64)[:, None] * freq[None, :]).astype(np.float32)
    cosine, sine = np.cos(angle.astype(np.float64)), np.sin(angle.astype(np.float64))
    rest = np.concatenate([cosine, cosine, -sine, sine], axis=1).astype(np.float32)
    terms = []
    for _ in range(3):
        term = rest.astype(jnp.bfloat16)
        terms.append(term)
        rest = rest - term.astype(np.float32)
    return np.stack(terms)


def fused_device(
    tokens,
    query_weight,
    adapter_down_weight,
    adapter_up_weight,
    row_adapter_index,
    adapter_table_slot,
    lengths,
    cached_key_rows,
    cached_value_rows,
):
    rows, features = tokens.shape
    columns = query_weight.shape[1]
    n_ad = lax.axis_size("ad")
    n_tp = lax.axis_size("tp")
    held = adapter_down_weight.shape[0]
    rank = adapter_down_weight.shape[2]
    _, kv_heads, span, head_dim = cached_key_rows.shape
    cap = -(-(384 // n_ad) // 16) * 16

    depth = 1024
    slot_count = 4
    swapped = SWAPPED
    chunk = CHUNK
    heads = columns // head_dim
    spread_rows = rows - swapped
    chunks = spread_rows // chunk
    kv_mine = kv_heads // n_tp
    group = heads // kv_mine
    pairs = rows // 2
    spread_pairs = spread_rows // 2
    width = columns // kv_mine
    vmem = pl.BlockSpec(memory_space=pltpu.VMEM)
    smem = pl.BlockSpec(memory_space=pltpu.SMEM)
    anywhere = pl.BlockSpec(memory_space=pl.ANY)
    bf16, f32 = jnp.bfloat16, jnp.float32
    dma = pltpu.SemaphoreType.DMA
    groups = n_ad // 2
    rope = rope_table(n_tp * span, head_dim)
    results = pl.pallas_call(
        functools.partial(step_kernel, n_ad, n_tp, cap, rank, swapped, chunk),
        out_shape=(jax.ShapeDtypeStruct((rows, columns), bf16),) * 2,
        in_specs=[vmem] * 3 + [smem] + [anywhere] * 7,
        out_specs=(anywhere, anywhere),
        scratch_shapes=[
            pltpu.VMEM((rows, features), bf16),
            pltpu.VMEM(rope.shape, bf16),
            pltpu.VMEM((rows, LANES), bf16),
            pltpu.VMEM((rows, n_ad * cap), bf16),
            pltpu.VMEM((rows, head_dim), f32),
            pltpu.VMEM((rows, head_dim), f32),
            pltpu.VMEM((n_ad, cap, features + LANES), bf16),
            pltpu.VMEM((n_tp, rows, features), bf16),
            pltpu.VMEM((n_ad, cap, features + LANES), bf16),
            pltpu.VMEM((groups, 2 * cap, held * rank), bf16),
            pltpu.VMEM((kv_mine, n_ad, cap, width), bf16),
            pltpu.VMEM((kv_mine, n_ad, cap, width), bf16),
            pltpu.VMEM((groups, cap, LANES), bf16),
            pltpu.VMEM((groups, n_tp, cap, LANES), bf16),
            pltpu.VMEM((rows, columns), f32),
            pltpu.VMEM((slot_count, depth, columns), bf16),
            pltpu.VMEM((held * rank, features), bf16),
            pltpu.VMEM((held * rank, columns), bf16),
            pltpu.VMEM((rows, columns), bf16),
            pltpu.VMEM((rows, columns), bf16),
            pltpu.VMEM((kv_mine, rows, group, head_dim), f32),
            pltpu.VMEM((kv_mine, pairs, 2 * group, head_dim), bf16),
            pltpu.VMEM((kv_mine, swapped, n_tp, span, head_dim), bf16),
            pltpu.VMEM((kv_mine, swapped, n_tp, span, head_dim), bf16),
            pltpu.VMEM((kv_mine, n_tp, spread_pairs, 2 * group, head_dim), bf16),
            pltpu.VMEM((kv_mine, spread_rows, n_tp, span, head_dim), bf16),
            pltpu.VMEM((kv_mine, spread_rows, n_tp, span, head_dim), bf16),
            pltpu.VMEM((kv_mine, n_tp, spread_pairs, 2 * group, head_dim), bf16),
            pltpu.VMEM((kv_mine, chunks, 2, group, LANES), f32),
            pltpu.VMEM((kv_mine, n_tp, spread_pairs, 2 * group, head_dim), bf16),
            pltpu.VMEM((kv_mine, chunks, n_tp, 2, group, LANES), f32),
            dma((slot_count,)),
            dma((4,)),
            dma((kv_mine, 2, n_tp + 1)),
            dma((2 * kv_mine + kv_mine * chunks,)),
            dma((n_tp, 2)),
            dma((n_tp, 2)),
            dma((n_ad,)),
            dma((n_ad,)),
            dma((groups, n_tp)),
            dma((groups, n_tp)),
            dma((kv_mine, n_ad)),
            dma((kv_mine, n_ad)),
            dma((2, kv_mine, n_tp)),
            dma((2, kv_mine, n_tp)),
            dma((kv_mine, chunks, n_tp)),
            dma((kv_mine, chunks, n_tp)),
            dma((kv_mine, chunks, n_tp)),
            dma((kv_mine, chunks, n_tp)),
            dma((kv_mine, chunks, n_tp)),
            dma((kv_mine, chunks, n_tp)),
        ],
        compiler_params=pltpu.CompilerParams(
            collective_id=0, has_side_effects=True, vmem_limit_bytes=60 * 1024 * 1024
        ),
        name="step",
    )(
        row_adapter_index[None, :],
        adapter_table_slot[None, :],
        lengths[None, :],
        lengths,
        tokens,
        jnp.asarray(rope),
        query_weight,
        adapter_down_weight.transpose(0, 2, 1).reshape(held * rank, features),
        adapter_up_weight.reshape(held * rank, columns),
        cached_key_rows,
        cached_value_rows,
    )
    return pl.pallas_call(
        hand_over,
        out_shape=(jax.ShapeDtypeStruct((rows, columns), bf16),) * 2,
        in_specs=[anywhere] * 2,
        out_specs=(anywhere, anywhere),
        scratch_shapes=[pltpu.VMEM((2, rows, columns), bf16), dma((2, 2))],
        name="hand_over",
    )(*results)


def rotate(query, lengths):
    head_dim = query.shape[-1]
    half = head_dim // 2
    freq = jnp.exp(jnp.arange(half, dtype=jnp.float32) * (-2.0 * math.log(500000.0) / head_dim))
    angle = (lengths - 1).astype(jnp.float32)[:, None, None] * freq[None, None, :]
    cosine = jnp.cos(angle)
    sine = jnp.sin(angle)
    first = query[..., :half]
    second = query[..., half:]
    return jnp.concatenate(
        [first * cosine - second * sine, second * cosine + first * sine], axis=-1
    )


def lookup(ids, adapter_table_slot):
    table = jnp.arange(adapter_table_slot.shape[0], dtype=jnp.int32)
    return jnp.sum(
        jnp.where(ids[:, None] == table[None, :], adapter_table_slot[None, :], 0), axis=1
    )


def shrink_rows(input_rows, local_partial, adapter_down_weight):
    adapter_row_count = adapter_down_weight.shape[0]
    select_rows = (
        local_partial[:, None] == jnp.arange(adapter_row_count, dtype=jnp.int32)[None, :]
    ).astype(jnp.float32)
    update_terms = jnp.einsum(
        "nt,vtm->nvm", input_rows, adapter_down_weight, preferred_element_type=jnp.float32
    )
    return (select_rows, jnp.sum(update_terms * select_rows[:, :, None], axis=1))


def expand_rows(select_rows, reduced_rows, adapter_up_weight):
    spread_rows = (select_rows[:, :, None] * reduced_rows.astype(jnp.float32)[:, None, :]).astype(
        jnp.bfloat16
    )
    return jnp.einsum(
        "pow,owu->pu", spread_rows, adapter_up_weight, preferred_element_type=jnp.float32
    ).astype(jnp.bfloat16)


def per_device(
    tokens,
    query_weight,
    adapter_down_weight,
    adapter_up_weight,
    row_adapter_index,
    adapter_table_slot,
    lengths,
    cached_key_rows,
    cached_value_rows,
):
    rows = tokens.shape[0]
    columns = query_weight.shape[1]
    tp_count = lax.axis_size("tp")
    owner_partials = adapter_down_weight.shape[0]
    base = jnp.dot(
        lax.all_gather(tokens, "tp", axis=1, tiled=True),
        query_weight,
        preferred_element_type=jnp.float32,
    )
    combined_output, every_id = (
        lax.all_gather(tokens, "ad", axis=0, tiled=True),
        lax.all_gather(row_adapter_index, "ad", axis=0, tiled=True),
    )
    slots = lookup(every_id, adapter_table_slot)
    mine = slots // owner_partials == lax.axis_index("ad")
    local_partial = jnp.where(mine, slots % owner_partials, -1)
    select_rows, partial_value_sum = shrink_rows(
        combined_output, local_partial, adapter_down_weight
    )
    reduced_rows = lax.psum(partial_value_sum, "tp").astype(jnp.bfloat16)
    lowrank_change = expand_rows(select_rows, reduced_rows, adapter_up_weight)
    delta = lax.psum_scatter(
        lowrank_change.astype(jnp.float32).astype(jnp.bfloat16),
        "ad",
        scatter_dimension=0,
        tiled=True,
    ).astype(jnp.float32)
    head_dim = cached_key_rows.shape[3]
    query = (base + delta).reshape(rows, columns // head_dim, head_dim)
    queries = rotate(query, lengths).reshape(rows, columns).astype(jnp.bfloat16)
    every_head = lax.all_gather(queries, "tp", axis=1, tiled=True)
    kv_heads = cached_key_rows.shape[1]
    span = cached_key_rows.shape[2]
    grouped = every_head.reshape(rows, kv_heads, -1, head_dim)
    scores = jnp.einsum(
        "rkgd,rkpd->rkgp", grouped, cached_key_rows, preferred_element_type=jnp.float32
    ) * (1.0 / math.sqrt(head_dim))
    position = lax.axis_index("tp") * span + jnp.arange(span, dtype=jnp.int32)
    valid = (position[None, :] < lengths[:, None])[:, None, None, :]
    scores = jnp.where(valid, scores, -1e30)
    peak = jnp.max(scores, axis=-1)
    weights = jnp.where(valid, jnp.exp(scores - peak[..., None]), 0.0)
    total = jnp.sum(weights, axis=-1)
    partial_out = jnp.einsum(
        "rkgp,rkpd->rkgd",
        weights.astype(jnp.bfloat16),
        cached_value_rows,
        preferred_element_type=jnp.float32,
    ).astype(jnp.bfloat16)
    peaks, totals = (
        lax.all_to_all(
            peak.reshape(rows, tp_count, -1), "tp", split_axis=1, concat_axis=1, tiled=True
        ),
        lax.all_to_all(
            total.reshape(rows, tp_count, -1), "tp", split_axis=1, concat_axis=1, tiled=True
        ),
    )
    partials = lax.all_to_all(
        partial_out.reshape(rows, tp_count, -1), "tp", split_axis=1, concat_axis=1, tiled=True
    )
    highest = jnp.max(peaks, axis=1, keepdims=True)
    factor = jnp.exp(peaks - highest)
    numer = jnp.sum(
        factor[..., None] * partials.reshape(rows, tp_count, -1, head_dim).astype(jnp.float32),
        axis=1,
    )
    denom = jnp.sum(factor * totals, axis=1)
    attended = (numer / denom[..., None]).reshape(rows, columns).astype(jnp.bfloat16)
    return (queries, attended)


def solution(mesh):
    fits = mesh.shape["tp"] == 4 and mesh.shape["ad"] == 8
    return jax.shard_map(
        fused_device if fits else per_device,
        mesh=mesh,
        in_specs=(
            P("ad", "tp"),
            P(None, "tp"),
            P("ad", "tp", None),
            P("ad", None, "tp"),
            P("ad"),
            P(),
            P("ad"),
            P("ad", None, "tp", None),
            P("ad", None, "tp", None),
        ),
        out_specs=(P("ad", "tp"), P("ad", "tp")),
        check_vma=False,
    )
```
